256 devices in a mesh: row: 32 (over z_lo, x, core), col: 8 (over z_hi, y).
Axes of the slice: x: 4, y: 4, z: 8 (z_hi: 2, z_lo: 4; z = z_hi * 4 + z_lo), core: 2. Of those that a mesh axis runs over, the one named last changes fastest.
Arguments:
- row_emb: bfloat16 [32768, 256], P('row'), may hold values from -1.5 to 1.5
- col_emb: bfloat16 [8192, 256], P('col'), may hold values from -1.5 to 1.5
- counts: int32 [2, 32768, 8192], P(None, 'row', 'col'), may hold values from 0 to 2025, as said below
- row_totals: int32 [32768], P('row'), may hold values from 1 to 4096
- col_totals: int32 [8192], P('col'), may hold values from 1 to 4096
- row_ids: int32 [2, 32768], replicated, may hold values from 0 to 32767, as said below
- col_ids: int32 [2, 8192], P(None, 'col'), may hold values from 0 to 8191, as said below
Outputs:
- grad_rows: float32 [32768, 256], P('row')
- grad_cols: float32 [8192, 256], P('col')
The draws below stay inside these ranges and needn't reach their ends.
Inputs may be any that keep to these rules, and one draw needn't show every extreme that they name: `row_ids`: for each step a permutation of 0 to 32767; position p of it holds an item whose id divided by 1024 (rounded down) equals p modulo 32768 / 1024. `col_ids`: for each step and each c, positions c * 1024 to (c + 1) * 1024 - 1 hold a permutation of the items c * 1024 to (c + 1) * 1024 - 1. `counts`: about half of the entries are zero.
All inputs are finite; a program needn't handle non-finite values.
Results may differ from the reference program's by a relative error of at most 0.0037.
Values may be sent and summed in bfloat16 or wider, within the bound.
A program may use at most 64 MiB of HBM per device.

```python
import math
import jax
import jax.numpy as jnp
from jax import lax

D = 256
BR = 1024
BC = 1024
STEPS = 2
NR = 32768
NC = 8192
N_ROW = 32
N_COL = 8


def draw_counts(key, part):
    shape = (STEPS, NR, NC)
    first = jax.random.fold_in(key, 11)
    second = jax.random.fold_in(key, 12)
    third = jax.random.fold_in(key, 13)
    present = jax.random.randint(first, shape, 0, 2)
    left = jax.random.randint(second, shape, 1, 46)
    right = jax.random.randint(third, shape, 1, 46)
    return (present * left * right).astype(jnp.int32)


def draw_row_totals(key, part):
    left = jax.random.randint(jax.random.fold_in(key, 21), (NR,), 1, 65)
    right = jax.random.randint(jax.random.fold_in(key, 22), (NR,), 1, 65)
    return (left * right).astype(jnp.int32)


def draw_col_totals(key, part):
    left = jax.random.randint(jax.random.fold_in(key, 31), (NC,), 1, 65)
    right = jax.random.randint(jax.random.fold_in(key, 32), (NC,), 1, 65)
    return (left * right).astype(jnp.int32)


def draw_row_ids(key, part):
    owners = NR // BR
    share = BR // owners
    keys = jax.random.split(jax.random.fold_in(key, 41), STEPS * owners)
    perms = jax.vmap(lambda single: jax.random.permutation(single, BR))(keys)
    perms = perms.reshape(STEPS, owners, owners, share)
    placed = jnp.transpose(perms, (0, 2, 3, 1)) + (jnp.arange(owners, dtype=jnp.int32) * BR)[None, None, None, :]
    return placed.reshape(STEPS, NR).astype(jnp.int32)


def draw_col_ids(key, part):
    blocks = NC // BC
    keys = jax.random.split(jax.random.fold_in(key, 51), STEPS * blocks)
    perms = jax.vmap(lambda single: jax.random.permutation(single, BC))(keys)
    perms = perms.reshape(STEPS, blocks, BC) + (jnp.arange(blocks, dtype=jnp.int32) * BC)[None, :, None]
    return perms.reshape(STEPS, NC).astype(jnp.int32)


def steps_of(key, dims, cuts, least, top_value):
    loudness = 1.0
    for position, parts in cuts:
        heights = jax.random.uniform(jax.random.fold_in(jax.random.fold_in(key, 6), position), (parts,), jnp.float32, least / len(cuts), top_value / len(cuts))
        loudness = loudness * jnp.repeat(jnp.exp(heights), dims[position] // parts).reshape((-1,) + (1,) * (len(dims) - 1 - position))
    return loudness


def bell_draw(key, dims, spread, bound, cuts=(), kind=jnp.bfloat16):
    level = steps_of(key, dims, cuts, -0.22, 0.18) if cuts else 1.0
    entries = jax.random.normal(key, dims, jnp.float32) * spread * level
    return jnp.minimum(jnp.maximum(entries, -bound), bound).astype(kind)


def setup_inputs(seed: int = 0) -> dict:
    arg_keys = jax.random.split(jax.random.key(seed), 8)
    return {
        "row_emb": bell_draw(arg_keys[0], (NR, D), 0.25, 1.5, ((0, 32),)),
        "col_emb": bell_draw(arg_keys[1], (NC, D), 0.25, 1.5, ((0, 8),)),
        "counts": draw_counts(jax.random.fold_in(arg_keys[7], 71), 0),
        "row_totals": draw_row_totals(jax.random.fold_in(arg_keys[7], 71), 0),
        "col_totals": draw_col_totals(jax.random.fold_in(arg_keys[7], 71), 0),
        "row_ids": draw_row_ids(jax.random.fold_in(arg_keys[7], 71), 0),
        "col_ids": draw_col_ids(jax.random.fold_in(arg_keys[7], 71), 0),
    }


log_total = 8.0

def block_slope(scores, block_counts, row_log, col_log):
    counted = block_counts.astype(jnp.float32)
    offset = log_total - row_log.astype(jnp.float32)[:, None] - col_log[None, :]
    fitted = (0.1 + 0.25 * jnp.sqrt(counted)) * (scores - jnp.log(jnp.maximum(counted, 1.0)) - offset)
    hinge = jax.nn.sigmoid(scores - offset)
    return jnp.where(block_counts > 0, fitted, hinge)

def reference(row_emb, col_emb, counts, row_totals, col_totals, row_ids, col_ids):
    row_log = jnp.log(row_totals.astype(jnp.float32)).astype(jnp.bfloat16)
    col_log = jnp.log(col_totals.astype(jnp.float32))
    scale = (STEPS * math.sqrt(NR * NC)) ** (-0.5)
    grad_rows = jnp.zeros((NR, D), jnp.float32)
    grad_cols = jnp.zeros((NC, D), jnp.float32)
    for step in range(STEPS):
        for block in range(N_ROW):
            rid = row_ids[step, block * BR:(block + 1) * BR]
            rows_here = row_emb[rid].astype(jnp.float32)
            for column in range(N_COL):
                cid = col_ids[step, column * BC:(column + 1) * BC]
                cols_here = col_emb[cid].astype(jnp.float32)
                scores = jnp.dot(rows_here, cols_here.T, precision=lax.Precision.HIGHEST)
                local = counts[step, block * BR:(block + 1) * BR, column * BC:(column + 1) * BC]
                slope = block_slope(scores, local, row_log[rid], col_log[cid])
                weights = (slope * scale).astype(jnp.bfloat16).astype(jnp.float32)
                grad_rows = grad_rows.at[rid].add(jnp.dot(weights, cols_here, precision=lax.Precision.HIGHEST))
                grad_cols = grad_cols.at[cid].add(jnp.dot(weights.T, rows_here, precision=lax.Precision.HIGHEST))
    return (grad_rows, grad_cols)
```

```python
import functools
import math

import jax
import jax.numpy as jnp
from jax import lax
from jax.experimental import pallas as pl
from jax.experimental.pallas import tpu as pltpu
from jax.sharding import PartitionSpec as P

MESH = pl.DeviceIdType.MESH
F32 = jnp.float32
BF16 = jnp.bfloat16
LOG_TOTAL = 8.0

S = 2
B = 1024
D = 256
NO = 32
NC = 8
T = 256
L = 128


def iota(shape, dim):
    return lax.broadcasted_iota(jnp.int32, shape, dim)


def nt(a, b):
    return lax.dot_general(a, b, (((1,), (1,)), ((), ())), preferred_element_type=F32)


def ds(start, size):
    return pl.ds(pl.multiple_of(start, size), size)


def kernel(
    scale,
    row_emb,
    col_emb,
    counts,
    row_tot,
    col_tot,
    want,
    want2,
    cid,
    out_rows,
    out_cols,
    cnt,
    idxcol,
    send,
    recv,
    logsend,
    logrecv,
    perm,
    rowsb,
    cols,
    rl,
    cl,
    score,
    wgt,
    rowterm,
    rowown,
    r1recv,
    racc,
    r2send,
    r2recv,
    r3x,
    r3send,
    big,
    xs,
    oh2,
    colt,
    gcol,
    c2send,
    c2recv,
    hacc,
    c3send,
    c3recv,
    c4acc,
    c4send,
    c4recv,
    colg,
    cnt_sem,
    f_send,
    f_recv,
    l_send,
    l_recv,
    r1_send,
    r1_recv,
    r2_send,
    r2_recv,
    r3_send,
    r3_recv,
    r4_send,
    r4_recv,
    c_send,
    c_recv,
):
    me = lax.axis_index("row")
    c = lax.axis_index("col")
    core = lax.rem(me, 2)
    x = lax.rem(lax.div(me, 2), 4)
    zl = lax.div(me, 8)
    zh = lax.div(c, 4)
    y = lax.rem(c, 4)
    pair = me + 1 - 2 * core
    other = (1 - zh) * 4 + y

    def row_of(zl_, x_, core_):
        return (zl_ * 4 + x_) * 2 + core_

    def remote(src, dst, send_sem, recv_sem, row, col):
        return pltpu.make_async_remote_copy(
            src_ref=src,
            dst_ref=dst,
            send_sem=send_sem,
            recv_sem=recv_sem,
            device_id={"row": row, "col": col},
            device_id_type=MESH,
        )

    def wait_bytes(ref, sem):
        pltpu.make_async_copy(ref, ref, sem).wait()

    for s in range(S):
        pltpu.make_async_copy(counts.at[s], cnt.at[s], cnt_sem.at[s]).start()

    barrier = pltpu.get_barrier_semaphore()

    def greet(d, carry):
        pl.semaphore_signal(
            barrier, inc=1, device_id={"row": lax.rem(me + d, NO), "col": c}, device_id_type=MESH
        )
        return carry

    lax.fori_loop(1, NO, greet, 0)
    for d in range(1, 4):
        pl.semaphore_signal(
            barrier,
            inc=1,
            device_id={"row": me, "col": zh * 4 + lax.rem(y + d, 4)},
            device_id_type=MESH,
        )
    pl.semaphore_signal(barrier, inc=1, device_id={"row": me, "col": other}, device_id_type=MESH)

    lane = iota((T, L), 1)
    sub = iota((T, L), 0)

    def fill_idx(ids):
        for b in range(8):
            idxcol[b * L : (b + 1) * L, :] = jnp.broadcast_to(ids[b : b + 1, :], (L, L)).T.astype(
                jnp.int32
            )

    def gather_tile(i, table, logs):
        ids = idxcol[ds(i * T, T), :]
        parts = []
        total = None
        for t in range(B // L):
            hit = ids == lane + t * L
            parts.append(jnp.where(hit, 1.0, 0.0).astype(BF16))
            entry = jnp.where(hit, logs[t : t + 1, :], 0.0)
            total = entry if total is None else total + entry
        picked = jnp.dot(jnp.concatenate(parts, axis=1), table[...], preferred_element_type=F32)
        return picked.astype(BF16), jnp.sum(total, axis=1, keepdims=True)

    row_logs = jnp.log(row_tot[...].astype(F32)).astype(BF16).astype(F32)
    logsend[...] = jnp.zeros_like(logsend)

    def make_send(s):
        fill_idx(want[s].astype(F32))

        def tile(i, carry):
            picked, column = gather_tile(i, row_emb, row_logs)
            send[s, ds(i * 8, 8)] = picked.reshape(8, 32, D)
            spread = jnp.where(lane == lax.rem(sub, 32), column, 0.0).reshape(8, 32, L)
            logsend[ds(i * 8, 8), s : s + 1, :] = jnp.sum(spread, axis=1, keepdims=True)
            return carry

        lax.fori_loop(0, B // T, tile, 0)

    def start_fetch(s):
        def one(d, carry):
            to = lax.rem(me + d, NO)
            remote(send.at[s, to], recv.at[s, me], f_send.at[s], f_recv.at[s], to, c).start()
            return carry

        lax.fori_loop(1, NO, one, 0)
        pltpu.make_async_copy(send.at[s, me], recv.at[s, me], f_recv.at[s]).start()

    def start_logs():
        def one(d, carry):
            to = lax.rem(me + d, NO)
            remote(logsend.at[to], logrecv.at[me], l_send, l_recv, to, c).start()
            return carry

        lax.fori_loop(1, NO, one, 0)
        pltpu.make_async_copy(logsend.at[me], logrecv.at[me], l_recv).start()

    make_send(0)
    pl.semaphore_wait(barrier, NO - 1 + 3 + 1)
    start_fetch(0)
    make_send(1)
    start_logs()

    col_logs = jnp.log(col_tot[...].astype(F32))
    for s in range(S):
        fill_idx(cid[s].astype(F32))

        def col_tile(i, carry, s=s):
            picked, column = gather_tile(i, col_emb, col_logs)
            cols[s, ds(i * T, T), :] = picked
            spread = jnp.where(lane == lax.rem(sub, L), column, 0.0).reshape(2, L, L)
            cl[s, ds(i * 2, 2)] = jnp.broadcast_to(
                jnp.sum(spread, axis=1, keepdims=True), (2, 8, L)
            )
            return carry

        lax.fori_loop(0, B // T, col_tile, 0)

    def perm_tile(i, carry):
        p = sub + i * T
        source = lax.rem(p, NO) * (B // NO) + lax.div(p, NO)
        parts = [jnp.where(source == lane + t * L, 1.0, 0.0).astype(BF16) for t in range(B // L)]
        perm[ds(i * T, T), :] = jnp.concatenate(parts, axis=1)
        return carry

    lax.fori_loop(0, B // T, perm_tile, 0)

    def oh2_tile(i, carry):
        for t in range(2 * B // L):
            hit = want2[t : t + 1, :] == sub + i * T
            oh2[ds(i * T, T), t * L : (t + 1) * L] = jnp.where(hit, 1.0, 0.0).astype(BF16)
        return carry

    lax.fori_loop(0, B // T, oh2_tile, 0)

    wait_bytes(logrecv, l_recv)
    for s in range(S):
        arrived = jnp.concatenate([logrecv[:, s, :], jnp.zeros((L - NO, L), F32)], axis=0).T
        spread = jnp.where(
            iota((NO, NO, L), 2) == iota((NO, NO, L), 1), arrived[:NO].reshape(NO, 1, L), 0.0
        )
        column = jnp.sum(spread, axis=2, keepdims=True) - LOG_TOTAL
        rl[s] = jnp.broadcast_to(column, (NO, NO, L)).reshape(B, L)

    gcol[...] = jnp.zeros_like(gcol)

    def block(s):
        colt[...] = jnp.zeros_like(colt)

        def tile(t, carry):
            i = lax.rem(y + 1 + t, 4)
            rows = jnp.dot(
                perm[ds(i * T, T), :], recv[s].reshape(B, D), preferred_element_type=F32
            ).astype(BF16)
            score[...] = nt(rows, cols[s])

            def chunk(k, carry):
                at = ds(k * 32, 32)
                here = ds(i * T + k * 32, 32)
                row_part = rl[s, here, :]
                for t8 in range(B // L):
                    lanes = slice(t8 * L, (t8 + 1) * L)
                    count = cnt[s, here, lanes]
                    counted = jnp.maximum(count.astype(F32), 1.0)
                    shifted = score[at, lanes] + (row_part + cl[s, t8, 0:1, :])
                    fitted = (0.1 * scale + (0.25 * scale) * (counted * lax.rsqrt(counted))) * (
                        shifted - jnp.log(counted)
                    )
                    hinge = 0.5 * scale + (0.5 * scale) * jnp.tanh(0.5 * shifted)
                    wgt[at, lanes] = jnp.where(count > 0, fitted, hinge).astype(BF16)
                return carry

            lax.fori_loop(0, T // 32, chunk, 0)
            weights = wgt[...]
            term = jnp.dot(weights, cols[s], preferred_element_type=F32)
            colt[...] += jnp.dot(rows.T, weights, preferred_element_type=F32)
            rowterm[s, ds(i * T, T), :] = term.astype(BF16)

            @pl.when(t < 3)
            def _():
                remote(
                    rowterm.at[s, ds(i * T, T), :],
                    r1recv.at[s, t],
                    r1_send.at[s],
                    r1_recv.at[s],
                    me,
                    zh * 4 + i,
                ).start()

            @pl.when(t == 3)
            def _():
                rowown[...] = term

            return carry

        lax.fori_loop(0, 4, tile, 0)

    def scatter_cols(s):
        high = colt[...].astype(BF16)
        low = (colt[...] - high.astype(F32)).astype(BF16)

        def tile(i, carry):
            parts = []
            for t in range(B // L):
                hit = cid[s, t : t + 1, :] == sub + i * T
                parts.append(jnp.where(hit, 1.0, 0.0).astype(BF16))
            onehot = jnp.concatenate(parts, axis=1)
            gcol[ds(i * T, T), :] += nt(onehot, high) + nt(onehot, low)
            return carry

        lax.fori_loop(0, B // T, tile, 0)

    def sum_rows(s):
        wait_bytes(r1recv.at[s], r1_recv.at[s])
        total = racc[s]
        for d in range(3):
            total = total + r1recv[s, d].astype(F32)
        racc[s] = total
        r2send[s] = racc[s, ds((1 - zh) * L, L), :].astype(BF16)
        remote(r2send.at[s], r2recv.at[s], r2_send.at[s], r2_recv.at[s], me, other).start()

    def half_rows(s):
        wait_bytes(r2recv.at[s], r2_recv.at[s])
        mine = (racc[s, ds(zh * L, L), :] + r2recv[s].astype(F32)).astype(BF16)
        for h in range(2):
            start = h * 256 + s * 128
            r3x[start : start + L, :] = mine[:, h * L : (h + 1) * L]

    wait_bytes(recv.at[0], f_recv.at[0])
    start_fetch(1)
    wait_bytes(cnt.at[0], cnt_sem.at[0])
    block(0)
    racc[0] = rowown[...]
    scatter_cols(0)
    wait_bytes(recv.at[1], f_recv.at[1])
    wait_bytes(cnt.at[1], cnt_sem.at[1])
    sum_rows(0)
    block(1)
    racc[1] = rowown[...]
    scatter_cols(1)

    c2send[...] = gcol[ds((1 - core) * 512, 512), :].astype(BF16)
    remote(c2send, c2recv, c_send.at[0], c_recv.at[0], pair, c).start()
    sum_rows(1)
    half_rows(0)

    wait_bytes(c2recv, c_recv.at[0])
    hacc[...] = gcol[ds(core * 512, 512), :] + c2recv[...].astype(F32)
    c3send[...] = hacc[...].astype(BF16)
    for d in range(1, 4):
        to = lax.rem(x + d, 4)
        remote(
            c3send.at[ds(to * 128, 128), :],
            c3recv.at[d - 1],
            c_send.at[1],
            c_recv.at[1],
            row_of(zl, to, core),
            c,
        ).start()

    half_rows(1)
    order = iota((512, 512), 0)
    source = lax.rem(order, 16) * 32 + lax.div(order, 16)
    sorter = jnp.where(source == iota((512, 512), 1), 1.0, 0.0).astype(BF16)
    r3send[...] = (
        jnp.dot(sorter, r3x[...], preferred_element_type=F32).astype(BF16).reshape(NO, 16, L)
    )

    def to_owner(d, carry):
        to = lax.rem(me + d, NO)
        remote(r3send.at[to], big.at[c, me], r3_send, r3_recv, to, c).start()
        return carry

    lax.fori_loop(1, NO, to_owner, 0)
    pltpu.make_async_copy(r3send.at[me], big.at[c, me], r3_recv).start()

    wait_bytes(c3recv, c_recv.at[1])
    c4acc[...] = (
        hacc[ds(x * 128, 128), :]
        + c3recv[0].astype(F32)
        + c3recv[1].astype(F32)
        + c3recv[2].astype(F32)
    )
    c4send[...] = c4acc[...].astype(BF16)
    for d in range(1, 4):
        to = lax.rem(zl + d, 4)
        remote(
            c4send.at[ds(to * 32, 32), :],
            c4recv.at[d - 1],
            c_send.at[2],
            c_recv.at[2],
            row_of(to, x, core),
            c,
        ).start()

    wait_bytes(big.at[c], r3_recv)
    remote(big.at[c], big.at[c], r4_send.at[0], r4_recv.at[0], me, other).start()
    for d in range(1, 4):
        remote(
            big.at[c], big.at[c], r4_send.at[1], r4_recv.at[1], me, zh * 4 + lax.rem(y + d, 4)
        ).start()

    wait_bytes(c4recv, c_recv.at[2])
    base = core * 512 + x * 128
    piece = ds(base + zl * 32, 32)
    colg[piece, :] = (
        c4acc[ds(zl * 32, 32), :]
        + c4recv[0].astype(F32)
        + c4recv[1].astype(F32)
        + c4recv[2].astype(F32)
    ).astype(BF16)
    for d in range(1, 4):
        to = row_of(lax.rem(zl + d, 4), x, core)
        remote(colg.at[piece, :], colg.at[piece, :], c_send.at[3], c_recv.at[3], to, c).start()

    wait_bytes(big.at[other], r4_recv.at[0])
    for d in range(1, 4):
        remote(
            big.at[other],
            big.at[other],
            r4_send.at[2],
            r4_recv.at[2],
            me,
            zh * 4 + lax.rem(y + d, 4),
        ).start()

    wait_bytes(colg.at[0:96, :], c_recv.at[3])
    quarter = ds(base, 128)
    for d in range(1, 4):
        to = row_of(zl, lax.rem(x + d, 4), core)
        remote(colg.at[quarter, :], colg.at[quarter, :], c_send.at[4], c_recv.at[4], to, c).start()
    wait_bytes(colg.at[0:384, :], c_recv.at[4])
    half = ds(core * 512, 512)
    remote(colg.at[half, :], colg.at[half, :], c_send.at[5], c_recv.at[5], pair, c).start()

    wait_bytes(big.at[0:3], r4_recv.at[1])
    wait_bytes(big.at[0:3], r4_recv.at[2])
    for q in range(NC):
        entries = big[q].astype(F32).reshape(NO, 2, 8, L)
        for h in range(2):
            xs[q * 256 : (q + 1) * 256, h * L : (h + 1) * L] = (
                entries[:, h].reshape(256, L).astype(BF16)
            )

    def out_tile(i, carry):
        out_rows[ds(i * T, T), :] = jnp.dot(
            oh2[ds(i * T, T), :], xs[...], preferred_element_type=F32
        )
        return carry

    lax.fori_loop(0, B // T, out_tile, 0)

    wait_bytes(colg.at[half, :], c_recv.at[5])
    out_cols[...] = colg[...].astype(F32)

    for s in range(S):
        wait_bytes(send.at[s, 0 : NO - 1], f_send.at[s])
        wait_bytes(r1recv.at[s], r1_send.at[s])
        wait_bytes(r2send.at[s], r2_send.at[s])
    wait_bytes(logsend.at[0 : NO - 1], l_send)
    wait_bytes(r3send.at[0 : NO - 1], r3_send)
    wait_bytes(big.at[0], r4_send.at[0])
    wait_bytes(big.at[0:3], r4_send.at[1])
    wait_bytes(big.at[0:3], r4_send.at[2])
    wait_bytes(c2send, c_send.at[0])
    wait_bytes(c3recv, c_send.at[1])
    wait_bytes(c4recv, c_send.at[2])
    wait_bytes(colg.at[0:96, :], c_send.at[3])
    wait_bytes(colg.at[0:384, :], c_send.at[4])
    wait_bytes(colg.at[0:512, :], c_send.at[5])


def local(row_emb, col_emb, counts, row_totals, col_totals, row_ids, col_ids):
    me = lax.axis_index("row")
    layout = row_ids.reshape(S, NO, B // NO, NO)
    wanted = lax.dynamic_index_in_dim(layout, me, axis=3, keepdims=False) - me * B
    want = wanted.reshape(S, 8, L)
    want2 = jnp.transpose(wanted.reshape(S, NO, 4, 2, 4), (3, 2, 1, 0, 4)).reshape(16, L)
    cid = (col_ids - lax.axis_index("col") * B).reshape(S, 8, L)
    scale = (S * math.sqrt(NO * B * NC * B)) ** (-0.5)
    vmem = pl.BlockSpec(memory_space=pltpu.VMEM)
    v = pltpu.VMEM
    dma = pltpu.SemaphoreType.DMA
    return pl.pallas_call(
        functools.partial(kernel, scale),
        out_shape=(jax.ShapeDtypeStruct((B, D), F32), jax.ShapeDtypeStruct((B, D), F32)),
        in_specs=[vmem, vmem, pl.BlockSpec(memory_space=pl.ANY)] + [vmem] * 5,
        out_specs=(vmem, vmem),
        scratch_shapes=[
            v((S, B, B), jnp.int32),
            v((B, L), jnp.int32),
            v((S, NO, NO, D), BF16),
            v((S, NO, NO, D), BF16),
            v((NO, 8, L), F32),
            v((NO, 8, L), F32),
            v((B, B), BF16),
            v((T, D), BF16),
            v((S, B, D), BF16),
            v((S, B, L), F32),
            v((S, 8, 8, L), F32),
            v((T, B), F32),
            v((T, B), BF16),
            v((S, B, D), BF16),
            v((T, D), F32),
            v((S, 3, T, D), BF16),
            v((S, T, D), F32),
            v((S, L, D), BF16),
            v((S, L, D), BF16),
            v((512, L), BF16),
            v((NO, 16, L), BF16),
            v((NC, NO, 16, L), BF16),
            v((2 * B, D), BF16),
            v((B, 2 * B), BF16),
            v((D, B), F32),
            v((B, D), F32),
            v((512, D), BF16),
            v((512, D), BF16),
            v((512, D), F32),
            v((512, D), BF16),
            v((3, 128, D), BF16),
            v((128, D), F32),
            v((128, D), BF16),
            v((3, 32, D), BF16),
            v((B, D), BF16),
            dma((S,)),
            dma((S,)),
            dma((S,)),
            dma,
            dma,
            dma((S,)),
            dma((S,)),
            dma((S,)),
            dma((S,)),
            dma,
            dma,
            dma((3,)),
            dma((3,)),
            dma((6,)),
            dma((6,)),
        ],
        compiler_params=pltpu.CompilerParams(
            collective_id=0, has_side_effects=True, vmem_limit_bytes=56 * 1024 * 1024
        ),
        name="swivel",
    )(
        row_emb,
        col_emb,
        counts,
        row_totals.reshape(8, L),
        col_totals.reshape(8, L),
        want,
        want2,
        cid,
    )


def solution(mesh):
    in_specs = (
        P("row", None),
        P("col", None),
        P(None, "row", "col"),
        P("row"),
        P("col"),
        P(),
        P(None, "col"),
    )
    out_specs = (P("row", None), P("col", None))
    return jax.shard_map(local, mesh=mesh, in_specs=in_specs, out_specs=out_specs, check_vma=False)
```

```python
import functools
import math

import jax
import jax.numpy as jnp
from jax import lax
from jax.experimental import pallas as pl
from jax.experimental.pallas import tpu as pltpu
from jax.sharding import PartitionSpec as P

MESH = pl.DeviceIdType.MESH
F32 = jnp.float32
BF16 = jnp.bfloat16
LOG_TOTAL = 8.0

S = 2
B = 1024
D = 256
NO = 32
NC = 8
T = 256
L = 128
VMEM_BYTES = 40 * 1024 * 1024


def iota(shape, dim):
    return lax.broadcasted_iota(jnp.int32, shape, dim)


def nt(a, b):
    return lax.dot_general(a, b, (((1,), (1,)), ((), ())), preferred_element_type=F32)


def ds(start, size):
    return pl.ds(pl.multiple_of(start, size), size)


def kernel(
    scale,
    row_emb,
    col_emb,
    counts,
    row_tot,
    col_tot,
    rid,
    cid_in,
    out_rows,
    out_cols,
    cnt,
    idxcol,
    cid,
    want,
    want2,
    send,
    recv,
    logsend,
    logrecv,
    sorter,
    unsort,
    cols,
    rl,
    cl,
    score,
    wgt,
    rowterm,
    rowown,
    r1recv,
    r2send,
    r2recv,
    r3x,
    r3send,
    big,
    xs,
    oh2,
    colt,
    gcol,
    c2send,
    c2recv,
    hacc,
    c3send,
    c3recv,
    c4acc,
    c4send,
    c4recv,
    colg,
    cnt_sem,
    f_send,
    f_recv,
    l_send,
    l_recv,
    r1_send,
    r1_recv,
    r2_send,
    r2_recv,
    r3_send,
    r3_recv,
    r4_send,
    r4_recv,
    c_send,
    c_recv,
):
    me = lax.axis_index("row")
    c = lax.axis_index("col")
    core = lax.rem(me, 2)
    x = lax.rem(lax.div(me, 2), 4)
    zl = lax.div(me, 8)
    zh = lax.div(c, 4)
    y = lax.rem(c, 4)
    z = zh * 4 + zl
    pair = me + 1 - 2 * core
    other = (1 - zh) * 4 + y

    def row_of(zl_, x_, core_):
        return (zl_ * 4 + x_) * 2 + core_

    def ring_peer(d):
        group = lax.div(d, 8)
        rest = lax.rem(d, 8)
        dz = jnp.where(
            group == 0, 0, jnp.where(group == 1, 1, jnp.where(group == 2, 7, 2 + 4 * core))
        )
        z2 = lax.rem(z + dz, 8)
        x2 = lax.rem(x + lax.div(rest, 2), 4)
        core2 = lax.rem(core + lax.rem(rest, 2), 2)
        return row_of(lax.rem(z2, 4), x2, core2), lax.div(z2, 4) * 4 + y

    def remote(src, dst, send_sem, recv_sem, row, col):
        return pltpu.make_async_remote_copy(
            src_ref=src,
            dst_ref=dst,
            send_sem=send_sem,
            recv_sem=recv_sem,
            device_id={"row": row, "col": col},
            device_id_type=MESH,
        )

    def wait_bytes(ref, sem):
        pltpu.make_async_copy(ref, ref, sem).wait()

    for s in range(S):
        pltpu.make_async_copy(counts.at[s], cnt.at[s], cnt_sem.at[s]).start()

    barrier = pltpu.get_barrier_semaphore()

    def signal(row, col):
        pl.semaphore_signal(
            barrier, inc=1, device_id={"row": row, "col": col}, device_id_type=MESH
        )

    def greet(d, carry):
        z2 = lax.rem(z + lax.div(d, 8) + 6, 8)
        x2 = lax.rem(x + lax.rem(lax.div(d, 2), 4), 4)
        core2 = lax.rem(core + lax.rem(d, 2), 2)
        signal(row_of(lax.rem(z2, 4), x2, core2), lax.div(z2, 4) * 4 + y)
        return carry

    lax.fori_loop(0, 16, greet, 0)
    lax.fori_loop(17, 40, greet, 0)
    for d in range(1, 4):
        signal(me, zh * 4 + lax.rem(y + d, 4))
        signal(row_of(lax.rem(zl + d, 4), x, core), c)
    signal(me, other)

    lane = iota((T, L), 1)
    sub = iota((T, L), 0)

    lane1 = iota((L, L), 1)
    sub1 = iota((L, L), 0)
    pick = jnp.where(sub1 == lax.rem(lane1, 4) * NO + me, 1.0, 0.0).astype(BF16)
    lane2 = iota((32, L), 1)
    sub2 = iota((32, L), 0)
    eighth = (
        lax.rem(y + 1 + lax.div(lax.rem(lane2, 32), 8), 4) * 2 + lax.div(lax.rem(lane2, 8), 4)
    )
    mask_want = jnp.where(
        (lax.div(sub2, 8) == lax.div(lane2, 32)) & (lax.rem(sub2, 8) == eighth), 1.0, 0.0
    )
    mask_want2 = jnp.where(iota((16, 1, L), 0) == lax.div(iota((16, 1, L), 2), 8), 1.0, 0.0)
    low_half = lax.rem(iota((1, L), 1), 8) < 4
    for s in range(S):
        ids = rid[s] - me * B
        high = jnp.right_shift(ids, 5).astype(F32).astype(BF16)
        low = jnp.bitwise_and(ids, 31).astype(F32).astype(BF16)
        picked_ids = 32.0 * jnp.dot(high, pick, preferred_element_type=F32) + jnp.dot(
            low, pick, preferred_element_type=F32
        )
        want[s] = jnp.sum(picked_ids.reshape(8, 32, L) * mask_want[None], axis=1)
        by_eighth = jnp.sum(picked_ids.reshape(2, 16, 8, L) * mask_want2[None], axis=1)
        for q in range(4):
            for half in range(2):
                want2[s, q * 2 + half : q * 2 + half + 1, :] = jnp.where(
                    low_half,
                    by_eighth[half, 2 * q : 2 * q + 1, :],
                    by_eighth[half, 2 * q + 1 : 2 * q + 2, :],
                ).astype(jnp.int32)
        cid[s] = (
            jnp.concatenate(
                [cid_in[s : s + 1, t * L : (t + 1) * L] for t in range(B // L)], axis=0
            )
            - c * B
        )

    def fill_idx(ids):
        for b in range(8):
            idxcol[b * L : (b + 1) * L, :] = jnp.broadcast_to(ids[b : b + 1, :], (L, L)).T.astype(
                jnp.int32
            )

    def gather_tile(i, table, logs):
        ids = idxcol[ds(i * T, T), :]
        parts = []
        total = None
        for t in range(B // L):
            hit = ids == lane + t * L
            parts.append(jnp.where(hit, 1.0, 0.0).astype(BF16))
            entry = jnp.where(hit, logs[t : t + 1, :], 0.0)
            total = entry if total is None else total + entry
        picked = jnp.dot(jnp.concatenate(parts, axis=1), table[...], preferred_element_type=F32)
        return picked, jnp.sum(total, axis=1, keepdims=True)

    row_logs = jnp.log(row_tot[...].astype(F32)).astype(BF16).astype(F32)
    col_logs = jnp.log(col_tot[...].astype(F32))

    def make_send(s):
        fill_idx(want[s])

        def tile(i, carry):
            picked, column = gather_tile(i, row_emb, row_logs)
            picked = picked.reshape(32, 8, D)
            packed = jnp.concatenate([picked[:, :, :L], picked[:, :, L:]], axis=1).astype(BF16)
            send[s, ds(i * 8, 8)] = packed.reshape(8, 4, 16, L)
            spread = jnp.where(lane == lax.rem(sub, 32), column, 0.0).reshape(8, 32, L)
            logsend[s, ds(i * 8, 8)] = jnp.sum(spread, axis=1, keepdims=True)
            return carry

        lax.fori_loop(0, B // T, tile, 0)

    def start_fetch(s):
        def one_log(d, carry):
            row, col = ring_peer(d)
            remote(
                logsend.at[s, row], logrecv.at[s, me], l_send.at[s], l_recv.at[s], row, col
            ).start()
            return carry

        lax.fori_loop(1, NO, one_log, 0)
        pltpu.make_async_copy(logsend.at[s, me], logrecv.at[s, me], l_recv.at[s]).start()
        for t in range(4):

            def one(d, carry, t=t):
                row, col = ring_peer(d)
                remote(
                    send.at[s, row, t],
                    recv.at[s, t, me],
                    f_send.at[s],
                    f_recv.at[s, t],
                    row,
                    col,
                ).start()
                return carry

            lax.fori_loop(1, NO, one, 0)
            pltpu.make_async_copy(send.at[s, me, t], recv.at[s, t, me], f_recv.at[s, t]).start()

    def make_cols(s):
        fill_idx(cid[s].astype(F32))

        def tile(i, carry):
            picked, column = gather_tile(i, col_emb, col_logs)
            cols[s, ds(i * T, T), :] = picked.astype(BF16)
            spread = jnp.where(lane == lax.rem(sub, L), column, 0.0).reshape(2, L, L)
            cl[s, ds(i * 2, 2)] = jnp.broadcast_to(
                jnp.sum(spread, axis=1, keepdims=True), (2, 8, L)
            )
            return carry

        lax.fori_loop(0, B // T, tile, 0)

    def make_row_logs(s):
        wait_bytes(logrecv.at[s], l_recv.at[s])
        arrived = jnp.concatenate(
            [logrecv[s].reshape(NO, L), jnp.zeros((L - NO, L), F32)], axis=0
        ).T
        spread = jnp.where(
            iota((NO, NO, L), 2) == iota((NO, NO, L), 1), arrived[:NO].reshape(NO, 1, L), 0.0
        )
        column = jnp.sum(spread, axis=2, keepdims=True) - LOG_TOTAL
        rl[s] = jnp.broadcast_to(column, (NO, NO, L)).reshape(B, L)

    def block_tile(s, t):
        i = lax.rem(y + 1 + t, 4)
        wait_bytes(recv.at[s, t], f_recv.at[s, t])
        arrived = jnp.dot(
            unsort[...], recv[s, t].reshape(512, L), preferred_element_type=F32
        ).astype(BF16)
        rows = jnp.concatenate([arrived[:T], arrived[T:]], axis=1)
        score[...] = nt(rows, cols[s])

        def chunk(k, carry):
            at = ds(k * 32, 32)
            here = ds(i * T + k * 32, 32)
            row_part = rl[s, ds(t * T + k * 32, 32), :]
            for t8 in range(B // L):
                lanes = slice(t8 * L, (t8 + 1) * L)
                count = cnt[s, here, lanes]
                counted = jnp.maximum(count.astype(F32), 1.0)
                shifted = score[at, lanes] + (row_part + cl[s, t8, 0:1, :])
                fitted = (0.1 * scale + (0.25 * scale) * (counted * lax.rsqrt(counted))) * (
                    shifted - jnp.log(counted)
                )
                hinge = 0.5 * scale + (0.5 * scale) * jnp.tanh(0.5 * shifted)
                wgt[at, lanes] = jnp.where(count > 0, fitted, hinge).astype(BF16)
            return carry

        lax.fori_loop(0, T // 32, chunk, 0)
        weights = wgt[...]
        term = jnp.dot(weights, cols[s], preferred_element_type=F32)
        colt[s] += jnp.dot(rows.T, weights, preferred_element_type=F32)
        rowterm[s, ds(i * T, T), :] = term.astype(BF16)

        @pl.when(t < 3)
        def _():
            remote(
                rowterm.at[s, ds(i * T, T), :],
                r1recv.at[s, t],
                r1_send.at[s],
                r1_recv.at[s],
                me,
                zh * 4 + i,
            ).start()

        @pl.when(t == 3)
        def _():
            rowown[...] = term

    def scatter_cols(s):
        high = colt[s].astype(BF16)
        low = (colt[s] - high.astype(F32)).astype(BF16)

        def tile(i, carry):
            parts = []
            for t in range(B // L):
                hit = cid[s, t : t + 1, :] == sub + i * T
                parts.append(jnp.where(hit, 1.0, 0.0).astype(BF16))
            onehot = jnp.concatenate(parts, axis=1)
            part = nt(onehot, high) + nt(onehot, low)
            if s == 0:
                gcol[ds(i * T, T), :] = part
            else:
                gcol[ds(i * T, T), :] += part
            return carry

        lax.fori_loop(0, B // T, tile, 0)

    def sum_over_y(s):
        wait_bytes(r1recv.at[s], r1_recv.at[s])
        total = rowown[...]
        for d in range(3):
            total = total + r1recv[s, d].astype(F32)
        r2send[s] = total.astype(BF16)
        remote(r2send.at[s], r2recv.at[s], r2_send.at[s], r2_recv.at[s], me, other).start()

    def to_owners(s):
        wait_bytes(r2recv.at[s], r2_recv.at[s])
        mine = (r2send[s].astype(F32) + r2recv[s].astype(F32)).astype(BF16)
        for h in range(2):
            r3x[h * T : (h + 1) * T, :] = mine[:, h * L : (h + 1) * L]
        r3send[s] = (
            jnp.dot(sorter[...], r3x[...], preferred_element_type=F32)
            .astype(BF16)
            .reshape(NO, 16, L)
        )

        def one(d, carry):
            row, col = ring_peer(d)
            remote(
                r3send.at[s, row], big.at[s, y, me], r3_send.at[s], r3_recv.at[s], row, col
            ).start()
            return carry

        lax.fori_loop(1, NO, one, 0)
        pltpu.make_async_copy(r3send.at[s, me], big.at[s, y, me], r3_recv.at[s]).start()

    def share_owned(s):
        wait_bytes(big.at[s, y], r3_recv.at[s])
        for d in range(1, 4):
            remote(
                big.at[s, y],
                big.at[s, y],
                r4_send.at[s],
                r4_recv.at[s],
                me,
                zh * 4 + lax.rem(y + d, 4),
            ).start()

    def make_oh2(s):
        def tile(i, carry):
            for t in range(B // L):
                hit = want2[s, t : t + 1, :] == sub + i * T
                oh2[s, ds(i * T, T), t * L : (t + 1) * L] = jnp.where(hit, 1.0, 0.0).astype(BF16)
            return carry

        lax.fori_loop(0, B // T, tile, 0)

    def add_rows(s):
        wait_bytes(big.at[s, 0:3], r4_recv.at[s])
        for q in range(4):
            entries = big[s, q].astype(F32).reshape(NO, 2, 8, L)
            for h in range(2):
                xs[q * T : (q + 1) * T, h * L : (h + 1) * L] = (
                    entries[:, h].reshape(T, L).astype(BF16)
                )

        def tile(i, carry):
            part = jnp.dot(oh2[s, ds(i * T, T), :], xs[...], preferred_element_type=F32)
            if s == 0:
                out_rows[ds(i * T, T), :] = part
            else:
                out_rows[ds(i * T, T), :] += part
            return carry

        lax.fori_loop(0, B // T, tile, 0)

    make_send(0)
    pl.semaphore_wait(barrier, 39 + 3 + 3 + 1)
    start_fetch(0)
    make_send(1)
    make_cols(0)
    order = iota((512, 512), 0)
    place = iota((512, 512), 1)
    sorter[...] = jnp.where(
        lax.rem(order, 16) * 32 + lax.div(order, 16) == place, 1.0, 0.0
    ).astype(BF16)
    unsort[...] = jnp.where(
        lax.rem(order, 32) * 16 + lax.div(order, 32) == place, 1.0, 0.0
    ).astype(BF16)
    colt[...] = jnp.zeros_like(colt)
    make_row_logs(0)
    wait_bytes(cnt.at[0], cnt_sem.at[0])

    def tile0(t, carry):
        block_tile(0, t)

        @pl.when(t == 0)
        def _():
            start_fetch(1)

        return carry

    lax.fori_loop(0, 4, tile0, 0)
    make_cols(1)
    make_row_logs(1)
    sum_over_y(0)
    wait_bytes(cnt.at[1], cnt_sem.at[1])

    def tile1(t, carry):
        @pl.when(t == 2)
        def _():
            to_owners(0)

        block_tile(1, t)
        return carry

    lax.fori_loop(0, 4, tile1, 0)
    sum_over_y(1)
    share_owned(0)
    scatter_cols(0)
    scatter_cols(1)

    c2send[...] = gcol[ds((1 - core) * 512, 512), :].astype(BF16)
    remote(c2send, c2recv, c_send.at[0], c_recv.at[0], pair, c).start()
    to_owners(1)

    wait_bytes(c2recv, c_recv.at[0])
    hacc[...] = gcol[ds(core * 512, 512), :] + c2recv[...].astype(F32)
    c3send[...] = hacc[...].astype(BF16)
    for d in range(1, 4):
        to = lax.rem(x + d, 4)
        remote(
            c3send.at[ds(to * 128, 128), :],
            c3recv.at[d - 1],
            c_send.at[1],
            c_recv.at[1],
            row_of(zl, to, core),
            c,
        ).start()
    make_oh2(0)

    wait_bytes(c3recv, c_recv.at[1])
    c4acc[...] = (
        hacc[ds(x * 128, 128), :]
        + c3recv[0].astype(F32)
        + c3recv[1].astype(F32)
        + c3recv[2].astype(F32)
    )
    c4send[...] = c4acc[...].astype(BF16)
    for d in range(1, 4):
        to = lax.rem(zl + d, 4)
        remote(
            c4send.at[ds(to * 32, 32), :],
            c4recv.at[d - 1],
            c_send.at[2],
            c_recv.at[2],
            row_of(to, x, core),
            c,
        ).start()
    make_oh2(1)

    wait_bytes(c4recv, c_recv.at[2])
    base = core * 512 + x * 128
    piece = ds(base + zl * 32, 32)
    colg[piece, :] = (
        c4acc[ds(zl * 32, 32), :]
        + c4recv[0].astype(F32)
        + c4recv[1].astype(F32)
        + c4recv[2].astype(F32)
    ).astype(BF16)
    for d in range(1, 4):
        to = row_of(lax.rem(zl + d, 4), x, core)
        remote(colg.at[piece, :], colg.at[piece, :], c_send.at[3], c_recv.at[3], to, c).start()

    share_owned(1)
    add_rows(0)

    wait_bytes(colg.at[0:96, :], c_recv.at[3])
    quarter = ds(base, 128)
    for d in range(1, 4):
        to = row_of(zl, lax.rem(x + d, 4), core)
        remote(colg.at[quarter, :], colg.at[quarter, :], c_send.at[4], c_recv.at[4], to, c).start()
    wait_bytes(colg.at[0:384, :], c_recv.at[4])
    half = ds(core * 512, 512)
    remote(colg.at[half, :], colg.at[half, :], c_send.at[5], c_recv.at[5], pair, c).start()

    add_rows(1)
    wait_bytes(colg.at[half, :], c_recv.at[5])
    out_cols[...] = colg[...].astype(F32)

    for s in range(S):
        wait_bytes(send.at[s, 0 : NO - 1], f_send.at[s])
        wait_bytes(logsend.at[s, 0 : NO - 1], l_send.at[s])
        wait_bytes(r1recv.at[s], r1_send.at[s])
        wait_bytes(r2send.at[s], r2_send.at[s])
        wait_bytes(r3send.at[s, 0 : NO - 1], r3_send.at[s])
        wait_bytes(big.at[s, 0:3], r4_send.at[s])
    wait_bytes(c2send, c_send.at[0])
    wait_bytes(c3recv, c_send.at[1])
    wait_bytes(c4recv, c_send.at[2])
    wait_bytes(colg.at[0:96, :], c_send.at[3])
    wait_bytes(colg.at[0:384, :], c_send.at[4])
    wait_bytes(colg.at[0:512, :], c_send.at[5])


def local(row_emb, col_emb, counts, row_totals, col_totals, row_ids, col_ids):
    scale = (S * math.sqrt(NO * B * NC * B)) ** (-0.5)
    vmem = pl.BlockSpec(memory_space=pltpu.VMEM)
    v = pltpu.VMEM
    dma = pltpu.SemaphoreType.DMA
    return pl.pallas_call(
        functools.partial(kernel, scale),
        out_shape=(jax.ShapeDtypeStruct((B, D), F32), jax.ShapeDtypeStruct((B, D), F32)),
        in_specs=[vmem, vmem, pl.BlockSpec(memory_space=pl.ANY)] + [vmem] * 4,
        out_specs=(vmem, vmem),
        scratch_shapes=[
            v((S, B, B), jnp.int32),
            v((B, L), jnp.int32),
            v((S, 8, L), jnp.int32),
            v((S, 8, L), F32),
            v((S, 8, L), jnp.int32),
            v((S, NO, 4, 16, L), BF16),
            v((S, 4, NO, 16, L), BF16),
            v((S, NO, 1, L), F32),
            v((S, NO, 1, L), F32),
            v((512, 512), BF16),
            v((512, 512), BF16),
            v((S, B, D), BF16),
            v((S, B, L), F32),
            v((S, 8, 8, L), F32),
            v((T, B), F32),
            v((T, B), BF16),
            v((S, B, D), BF16),
            v((T, D), F32),
            v((S, 3, T, D), BF16),
            v((S, T, D), BF16),
            v((S, T, D), BF16),
            v((512, L), BF16),
            v((S, NO, 16, L), BF16),
            v((S, 4, NO, 16, L), BF16),
            v((B, D), BF16),
            v((S, B, B), BF16),
            v((S, D, B), F32),
            v((B, D), F32),
            v((512, D), BF16),
            v((512, D), BF16),
            v((512, D), F32),
            v((512, D), BF16),
            v((3, 128, D), BF16),
            v((128, D), F32),
            v((128, D), BF16),
            v((3, 32, D), BF16),
            v((B, D), BF16),
            dma((S,)),
            dma((S,)),
            dma((S, 4)),
            dma((S,)),
            dma((S,)),
            dma((S,)),
            dma((S,)),
            dma((S,)),
            dma((S,)),
            dma((S,)),
            dma((S,)),
            dma((S,)),
            dma((S,)),
            dma((6,)),
            dma((6,)),
        ],
        compiler_params=pltpu.CompilerParams(
            collective_id=0, has_side_effects=True, vmem_limit_bytes=VMEM_BYTES
        ),
        name="swivel",
    )(
        row_emb,
        col_emb,
        counts,
        row_totals.reshape(8, L),
        col_totals.reshape(8, L),
        row_ids.reshape(S, NO * B // L, L),
        col_ids,
    )


def solution(mesh):
    in_specs = (
        P("row", None),
        P("col", None),
        P(None, "row", "col"),
        P("row"),
        P("col"),
        P(),
        P(None, "col"),
    )
    out_specs = (P("row", None), P("col", None))
    return jax.shard_map(local, mesh=mesh, in_specs=in_specs, out_specs=out_specs, check_vma=False)
```

```python
import functools
import math

import jax
import jax.numpy as jnp
from jax import lax
from jax.experimental import pallas as pl
from jax.experimental.pallas import tpu as pltpu
from jax.sharding import PartitionSpec as P

MESH = pl.DeviceIdType.MESH
F32 = jnp.float32
BF16 = jnp.bfloat16
LOG_TOTAL = 8.0

S = 2
B = 1024
D = 256
NO = 32
NC = 8
T = 256
L = 128
PIECES = 4
VMEM_BYTES = 57 * 1024 * 1024


def iota(shape, dim):
    return lax.broadcasted_iota(jnp.int32, shape, dim)


def nt(a, b):
    return lax.dot_general(a, b, (((1,), (1,)), ((), ())), preferred_element_type=F32)


def ds(start, size):
    return pl.ds(pl.multiple_of(start, size), size)


def kernel(
    scale,
    row_emb_hbm,
    col_emb_hbm,
    counts,
    row_tot_hbm,
    col_tot_hbm,
    rid_hbm,
    cid_hbm,
    out_rows,
    out_cols,
    row_emb,
    col_emb,
    row_tot,
    col_tot,
    rid,
    cid_in,
    cnt,
    idxcol,
    cid,
    want,
    want2,
    send,
    recv,
    logsend,
    logrecv,
    sorter,
    unsort,
    cols,
    rl,
    cl,
    score,
    wgt,
    rowterm,
    rowown,
    r1recv,
    r2send,
    r2recv,
    r3x,
    r3send,
    big,
    xs,
    oh2,
    ohc,
    colt,
    gcol,
    c2send,
    c2recv,
    hacc,
    c3send,
    c3recv,
    c4buf,
    colg,
    in_sem,
    cnt_sem,
    f_send,
    f_recv,
    l_send,
    l_recv,
    r1_send,
    r1_recv,
    r2_send,
    r2_recv,
    r3_send,
    r3_recv,
    r4_send,
    r4_recv,
    c_send,
    c_recv,
):
    me = lax.axis_index("row")
    c = lax.axis_index("col")
    core = lax.rem(me, 2)
    x = lax.rem(lax.div(me, 2), 4)
    zl = lax.div(me, 8)
    zh = lax.div(c, 4)
    y = lax.rem(c, 4)
    z = zh * 4 + zl
    pair = me + 1 - 2 * core
    other = (1 - zh) * 4 + y

    def row_of(zl_, x_, core_):
        return (zl_ * 4 + x_) * 2 + core_

    def ring_peer(d):
        group = lax.div(d, 8)
        rest = lax.rem(d, 8)
        dz = jnp.where(
            group == 0, 0, jnp.where(group == 1, 1, jnp.where(group == 2, 7, 2 + 4 * core))
        )
        z2 = lax.rem(z + dz, 8)
        x2 = lax.rem(x + lax.div(rest, 2), 4)
        core2 = lax.rem(core + lax.rem(rest, 2), 2)
        return row_of(lax.rem(z2, 4), x2, core2), lax.div(z2, 4) * 4 + y

    def remote(src, dst, send_sem, recv_sem, row, col):
        return pltpu.make_async_remote_copy(
            src_ref=src,
            dst_ref=dst,
            send_sem=send_sem,
            recv_sem=recv_sem,
            device_id={"row": row, "col": col},
            device_id_type=MESH,
        )

    def wait_bytes(ref, sem):
        pltpu.make_async_copy(ref, ref, sem).wait()

    loads = [
        pltpu.make_async_copy(src, dst, in_sem.at[k])
        for k, (src, dst) in enumerate(
            (
                (rid_hbm, rid),
                (row_tot_hbm, row_tot),
                (cid_hbm, cid_in),
                (col_tot_hbm, col_tot),
                (row_emb_hbm, row_emb),
                (col_emb_hbm, col_emb),
            )
        )
    ]
    for load in loads:
        load.start()
    for s in range(S):
        pltpu.make_async_copy(counts.at[s], cnt.at[s], cnt_sem.at[s]).start()

    barrier = pltpu.get_barrier_semaphore()

    def signal(row, col):
        pl.semaphore_signal(
            barrier, inc=1, device_id={"row": row, "col": col}, device_id_type=MESH
        )

    def greet(d, carry):
        z2 = lax.rem(z + lax.div(d, 8) + 6, 8)
        x2 = lax.rem(x + lax.rem(lax.div(d, 2), 4), 4)
        core2 = lax.rem(core + lax.rem(d, 2), 2)
        signal(row_of(lax.rem(z2, 4), x2, core2), lax.div(z2, 4) * 4 + y)
        return carry

    lax.fori_loop(0, 16, greet, 0)
    lax.fori_loop(17, 40, greet, 0)
    for d in range(1, 4):
        signal(me, zh * 4 + lax.rem(y + d, 4))
        signal(row_of(lax.rem(zl + d, 4), x, core), c)
    signal(me, other)

    lane = iota((T, L), 1)
    sub = iota((T, L), 0)

    lane1 = iota((L, L), 1)
    sub1 = iota((L, L), 0)
    pick = jnp.where(sub1 == lax.rem(lane1, 4) * NO + me, 1.0, 0.0).astype(BF16)
    lane2 = iota((32, L), 1)
    sub2 = iota((32, L), 0)
    eighth = (
        lax.rem(y + 1 + lax.div(lax.rem(lane2, 32), 8), 4) * 2 + lax.div(lax.rem(lane2, 8), 4)
    )
    mask_want = jnp.where(
        (lax.div(sub2, 8) == lax.div(lane2, 32)) & (lax.rem(sub2, 8) == eighth), 1.0, 0.0
    )
    mask_want2 = jnp.where(iota((16, 1, L), 0) == lax.div(iota((16, 1, L), 2), 8), 1.0, 0.0)
    low_half = lax.rem(iota((1, L), 1), 8) < 4
    for load in loads[:4]:
        load.wait()
    for s in range(S):
        ids = rid[s] - me * B
        high = jnp.right_shift(ids, 5).astype(F32).astype(BF16)
        low = jnp.bitwise_and(ids, 31).astype(F32).astype(BF16)
        picked_ids = 32.0 * jnp.dot(high, pick, preferred_element_type=F32) + jnp.dot(
            low, pick, preferred_element_type=F32
        )
        want[s] = jnp.sum(picked_ids.reshape(8, 32, L) * mask_want[None], axis=1)
        by_eighth = jnp.sum(picked_ids.reshape(2, 16, 8, L) * mask_want2[None], axis=1)
        for q in range(4):
            for half in range(2):
                want2[s, q * 2 + half : q * 2 + half + 1, :] = jnp.where(
                    low_half,
                    by_eighth[half, 2 * q : 2 * q + 1, :],
                    by_eighth[half, 2 * q + 1 : 2 * q + 2, :],
                ).astype(jnp.int32)
        cid[s] = (
            jnp.concatenate(
                [cid_in[s : s + 1, t * L : (t + 1) * L] for t in range(B // L)], axis=0
            )
            - c * B
        )

    def fill_idx(ids):
        for b in range(8):
            idxcol[b * L : (b + 1) * L, :] = jnp.broadcast_to(ids[b : b + 1, :], (L, L)).T.astype(
                jnp.int32
            )

    def gather_tile(i, table, logs):
        ids = idxcol[ds(i * T, T), :]
        parts = []
        total = None
        for t in range(B // L):
            hit = ids == lane + t * L
            parts.append(jnp.where(hit, 1.0, 0.0).astype(BF16))
            entry = jnp.where(hit, logs[t : t + 1, :], 0.0)
            total = entry if total is None else total + entry
        onehot = jnp.concatenate(parts, axis=1)
        picked = jnp.dot(onehot, table[...], preferred_element_type=F32)
        return picked, jnp.sum(total, axis=1, keepdims=True), onehot

    row_logs = jnp.log(row_tot[...].astype(F32)).astype(BF16).astype(F32)
    col_logs = jnp.log(col_tot[...].astype(F32))

    def make_send(s):
        fill_idx(want[s])

        def tile(i, carry):
            picked, column, _ = gather_tile(i, row_emb, row_logs)
            picked = picked.reshape(32, 8, D)
            packed = jnp.concatenate([picked[:, :, :L], picked[:, :, L:]], axis=1).astype(BF16)
            send[s, ds(i * 8, 8)] = packed.reshape(8, 4, 16, L)
            spread = jnp.where(lane == lax.rem(sub, 32), column, 0.0).reshape(8, 32, L)
            logsend[s, ds(i * 8, 8)] = jnp.sum(spread, axis=1, keepdims=True)
            return carry

        lax.fori_loop(0, B // T, tile, 0)

    def start_fetch(s):
        def one_log(d, carry):
            row, col = ring_peer(d)
            remote(
                logsend.at[s, row], logrecv.at[s, me], l_send.at[s], l_recv.at[s], row, col
            ).start()
            return carry

        lax.fori_loop(1, NO, one_log, 0)
        pltpu.make_async_copy(logsend.at[s, me], logrecv.at[s, me], l_recv.at[s]).start()
        for t in range(4):

            def one(d, carry, t=t):
                row, col = ring_peer(d)
                remote(
                    send.at[s, row, t],
                    recv.at[s, t, me],
                    f_send.at[s],
                    f_recv.at[s, t],
                    row,
                    col,
                ).start()
                return carry

            lax.fori_loop(1, NO, one, 0)
            pltpu.make_async_copy(send.at[s, me, t], recv.at[s, t, me], f_recv.at[s, t]).start()

    def make_cols(s):
        fill_idx(cid[s].astype(F32))

        def tile(i, carry):
            picked, column, onehot = gather_tile(i, col_emb, col_logs)
            ohc[s, ds(i * T, T), :] = onehot
            cols[s, ds(i * T, T), :] = picked.astype(BF16)
            spread = jnp.where(lane == lax.rem(sub, L), column, 0.0).reshape(2, L, L)
            cl[s, ds(i * 2, 2)] = jnp.broadcast_to(
                jnp.sum(spread, axis=1, keepdims=True), (2, 8, L)
            )
            return carry

        lax.fori_loop(0, B // T, tile, 0)

    def make_row_logs(s):
        wait_bytes(logrecv.at[s], l_recv.at[s])
        arrived = jnp.concatenate(
            [logrecv[s].reshape(NO, L), jnp.zeros((L - NO, L), F32)], axis=0
        ).T
        spread = jnp.where(
            iota((NO, NO, L), 2) == iota((NO, NO, L), 1), arrived[:NO].reshape(NO, 1, L), 0.0
        )
        column = jnp.sum(spread, axis=2, keepdims=True) - LOG_TOTAL
        rl[s] = jnp.broadcast_to(column, (NO, NO, L)).reshape(B, L)

    def block_tile(s, t):
        i = lax.rem(y + 1 + t, 4)
        wait_bytes(recv.at[s, t], f_recv.at[s, t])
        arrived = jnp.dot(
            unsort[...], recv[s, t].reshape(512, L), preferred_element_type=F32
        ).astype(BF16)
        rows = jnp.concatenate([arrived[:T], arrived[T:]], axis=1)
        score[...] = nt(rows, cols[s])

        def chunk(k, carry):
            at = ds(k * 32, 32)
            here = ds(i * T + k * 32, 32)
            row_part = rl[s, ds(t * T + k * 32, 32), :]
            for t8 in range(B // L):
                lanes = slice(t8 * L, (t8 + 1) * L)
                count = cnt[s, here, lanes]
                counted = jnp.maximum(count.astype(F32), 1.0)
                shifted = score[at, lanes] + (row_part + cl[s, t8, 0:1, :])
                fitted = (0.1 * scale + (0.25 * scale) * (counted * lax.rsqrt(counted))) * (
                    shifted - jnp.log(counted)
                )
                hinge = 0.5 * scale + (0.5 * scale) * jnp.tanh(0.5 * shifted)
                wgt[at, lanes] = jnp.where(count > 0, fitted, hinge).astype(BF16)
            return carry

        lax.fori_loop(0, T // 32, chunk, 0)
        weights = wgt[...]
        term = jnp.dot(weights, cols[s], preferred_element_type=F32)
        colt[s] += jnp.dot(rows.T, weights, preferred_element_type=F32)
        rowterm[s, ds(i * T, T), :] = term.astype(BF16)

        @pl.when(t < 3)
        def _():
            remote(
                rowterm.at[s, ds(i * T, T), :],
                r1recv.at[s, t],
                r1_send.at[s],
                r1_recv.at[s],
                me,
                zh * 4 + i,
            ).start()

        @pl.when(t == 3)
        def _():
            rowown[...] = term

    def scatter_cols():
        first = colt[0].astype(BF16)
        second = colt[1].astype(BF16)
        for n in range(B // T):
            lanes = slice(n * T, (n + 1) * T)
            part = jnp.dot(first, ohc[0, :, lanes], preferred_element_type=F32) + jnp.dot(
                second, ohc[1, :, lanes], preferred_element_type=F32
            )
            gcol[2 * n] = part[:, :L]
            gcol[2 * n + 1] = part[:, L:]

    def sum_over_y(s):
        wait_bytes(r1recv.at[s], r1_recv.at[s])
        total = rowown[...]
        for d in range(3):
            total = total + r1recv[s, d].astype(F32)
        r2send[s] = total.astype(BF16)
        remote(r2send.at[s], r2recv.at[s], r2_send.at[s], r2_recv.at[s], me, other).start()

    def to_owners(s):
        wait_bytes(r2recv.at[s], r2_recv.at[s])
        mine = (r2send[s].astype(F32) + r2recv[s].astype(F32)).astype(BF16)
        for h in range(2):
            r3x[h * T : (h + 1) * T, :] = mine[:, h * L : (h + 1) * L]
        r3send[s] = (
            jnp.dot(sorter[...], r3x[...], preferred_element_type=F32)
            .astype(BF16)
            .reshape(NO, 16, L)
        )

        def one(d, carry):
            row, col = ring_peer(d)
            remote(
                r3send.at[s, row], big.at[s, y, me], r3_send.at[s], r3_recv.at[s], row, col
            ).start()
            return carry

        lax.fori_loop(1, NO, one, 0)
        pltpu.make_async_copy(r3send.at[s, me], big.at[s, y, me], r3_recv.at[s]).start()

    def share_owned(s):
        wait_bytes(big.at[s, y], r3_recv.at[s])
        for d in range(1, 4):
            remote(
                big.at[s, y],
                big.at[s, y],
                r4_send.at[s],
                r4_recv.at[s],
                me,
                zh * 4 + lax.rem(y + d, 4),
            ).start()

    def make_oh2(s):
        def tile(i, carry):
            for t in range(B // L):
                hit = want2[s, t : t + 1, :] == sub + i * T
                oh2[s, ds(i * T, T), t * L : (t + 1) * L] = jnp.where(hit, 1.0, 0.0).astype(BF16)
            return carry

        lax.fori_loop(0, B // T, tile, 0)

    def add_rows(s):
        wait_bytes(big.at[s, 0:3], r4_recv.at[s])
        for q in range(4):
            entries = big[s, q].astype(F32).reshape(NO, 2, 8, L)
            for h in range(2):
                xs[q * T : (q + 1) * T, h * L : (h + 1) * L] = (
                    entries[:, h].reshape(T, L).astype(BF16)
                )

        def tile(i, carry):
            part = jnp.dot(oh2[s, ds(i * T, T), :], xs[...], preferred_element_type=F32)
            if s == 0:
                out_rows[ds(i * T, T), :] = part
            else:
                out_rows[ds(i * T, T), :] += part
            return carry

        lax.fori_loop(0, B // T, tile, 0)

    loads[4].wait()
    make_send(0)
    pl.semaphore_wait(barrier, 39 + 3 + 3 + 1)
    start_fetch(0)
    make_send(1)
    loads[5].wait()
    make_cols(0)
    order = iota((512, 512), 0)
    place = iota((512, 512), 1)
    sorter[...] = jnp.where(
        lax.rem(order, 16) * 32 + lax.div(order, 16) == place, 1.0, 0.0
    ).astype(BF16)
    unsort[...] = jnp.where(
        lax.rem(order, 32) * 16 + lax.div(order, 32) == place, 1.0, 0.0
    ).astype(BF16)
    colt[...] = jnp.zeros_like(colt)
    make_row_logs(0)
    wait_bytes(cnt.at[0], cnt_sem.at[0])

    def tile0(t, carry):
        block_tile(0, t)

        @pl.when(t == 0)
        def _():
            start_fetch(1)

        return carry

    lax.fori_loop(0, 4, tile0, 0)
    make_cols(1)
    make_row_logs(1)
    sum_over_y(0)
    wait_bytes(cnt.at[1], cnt_sem.at[1])

    def tile1(t, carry):
        @pl.when(t == 3)
        def _():
            to_owners(0)

        block_tile(1, t)
        return carry

    lax.fori_loop(0, 4, tile1, 0)
    sum_over_y(1)
    scatter_cols()

    c2send[...] = gcol[pl.ds(4 * (1 - core), 4)].astype(BF16)
    remote(c2send, c2recv, c_send.at[0], c_recv.at[0], pair, c).start()
    share_owned(0)

    wait_bytes(c2recv, c_recv.at[0])
    hacc[...] = gcol[pl.ds(4 * core, 4)] + c2recv[...].astype(F32)
    c3send[...] = hacc[...].astype(BF16)
    for d in range(1, 4):
        to = lax.rem(x + d, 4)
        remote(
            c3send.at[to], c3recv.at[d - 1], c_send.at[1], c_recv.at[1], row_of(zl, to, core), c
        ).start()
    make_oh2(0)
    to_owners(1)

    wait_bytes(c3recv, c_recv.at[1])
    c4buf[zl] = (
        hacc[x] + c3recv[0].astype(F32) + c3recv[1].astype(F32) + c3recv[2].astype(F32)
    ).astype(BF16)
    for d in range(1, 4):
        to = row_of(lax.rem(zl + d, 4), x, core)
        remote(c4buf.at[zl], c4buf.at[zl], c_send.at[2], c_recv.at[2], to, c).start()
    make_oh2(1)
    add_rows(0)
    share_owned(1)

    wait_bytes(c4buf.at[0:3], c_recv.at[2])
    total = (c4buf[0].astype(F32) + c4buf[1].astype(F32)) + (
        c4buf[2].astype(F32) + c4buf[3].astype(F32)
    )
    quarter = ds(core * 512 + x * 128, 128)
    colg[quarter, :] = total.T.astype(BF16)
    for d in range(1, 4):
        to = row_of(zl, lax.rem(x + d, 4), core)
        remote(colg.at[quarter, :], colg.at[quarter, :], c_send.at[3], c_recv.at[3], to, c).start()
    wait_bytes(colg.at[0:384, :], c_recv.at[3])
    half = ds(core * 512, 512)
    remote(colg.at[half, :], colg.at[half, :], c_send.at[4], c_recv.at[4], pair, c).start()

    add_rows(1)
    wait_bytes(colg.at[half, :], c_recv.at[4])
    out_cols[...] = colg[...]

    for s in range(S):
        wait_bytes(send.at[s, 0 : NO - 1], f_send.at[s])
        wait_bytes(logsend.at[s, 0 : NO - 1], l_send.at[s])
        wait_bytes(r1recv.at[s], r1_send.at[s])
        wait_bytes(r2send.at[s], r2_send.at[s])
        wait_bytes(r3send.at[s, 0 : NO - 1], r3_send.at[s])
        wait_bytes(big.at[s, 0:3], r4_send.at[s])
    wait_bytes(c2send, c_send.at[0])
    wait_bytes(c3recv, c_send.at[1])
    wait_bytes(c4buf.at[0:3], c_send.at[2])
    wait_bytes(colg.at[0:384, :], c_send.at[3])
    wait_bytes(colg.at[0:512, :], c_send.at[4])


def finish(rows, cols, out_rows, out_cols, rows_buf, cols_buf, wide, sem):
    size = B // PIECES
    pieces = [pl.ds(k * size, size) for k in range(PIECES)]
    moves = []
    for k, at in enumerate(pieces):
        moves.append(
            (
                pltpu.make_async_copy(cols.at[at], cols_buf.at[at], sem.at[k, 0]),
                pltpu.make_async_copy(rows.at[at], rows_buf.at[at], sem.at[k, 1]),
                pltpu.make_async_copy(wide.at[at], out_cols.at[at], sem.at[k, 2]),
                pltpu.make_async_copy(rows_buf.at[at], out_rows.at[at], sem.at[k, 3]),
            )
        )
    for move in moves:
        move[0].start()
        move[1].start()
    for k, move in enumerate(moves):
        move[0].wait()
        wide[pieces[k], :] = cols_buf[pieces[k], :].astype(F32)
        move[2].start()
        move[1].wait()
        move[3].start()
    for move in moves:
        move[2].wait()
        move[3].wait()


def local(row_emb, col_emb, counts, row_totals, col_totals, row_ids, col_ids):
    scale = (S * math.sqrt(NO * B * NC * B)) ** (-0.5)
    vmem = pl.BlockSpec(memory_space=pltpu.VMEM)
    hbm = pl.BlockSpec(memory_space=pl.ANY)
    v = pltpu.VMEM
    dma = pltpu.SemaphoreType.DMA
    rows, cols = pl.pallas_call(
        functools.partial(kernel, scale),
        out_shape=(jax.ShapeDtypeStruct((B, D), F32), jax.ShapeDtypeStruct((B, D), BF16)),
        in_specs=[hbm] * 7,
        out_specs=(vmem, vmem),
        scratch_shapes=[
            v((B, D), BF16),
            v((B, D), BF16),
            v((8, L), jnp.int32),
            v((8, L), jnp.int32),
            v((S, NO * B // L, L), jnp.int32),
            v((S, B), jnp.int32),
            v((S, B, B), jnp.int32),
            v((B, L), jnp.int32),
            v((S, 8, L), jnp.int32),
            v((S, 8, L), F32),
            v((S, 8, L), jnp.int32),
            v((S, NO, 4, 16, L), BF16),
            v((S, 4, NO, 16, L), BF16),
            v((S, NO, 1, L), F32),
            v((S, NO, 1, L), F32),
            v((512, 512), BF16),
            v((512, 512), BF16),
            v((S, B, D), BF16),
            v((S, B, L), F32),
            v((S, 8, 8, L), F32),
            v((T, B), F32),
            v((T, B), BF16),
            v((S, B, D), BF16),
            v((T, D), F32),
            v((S, 3, T, D), BF16),
            v((S, T, D), BF16),
            v((S, T, D), BF16),
            v((512, L), BF16),
            v((S, NO, 16, L), BF16),
            v((S, 4, NO, 16, L), BF16),
            v((B, D), BF16),
            v((S, B, B), BF16),
            v((S, B, B), BF16),
            v((S, D, B), F32),
            v((8, D, L), F32),
            v((4, D, L), BF16),
            v((4, D, L), BF16),
            v((4, D, L), F32),
            v((4, D, L), BF16),
            v((3, D, L), BF16),
            v((4, D, L), BF16),
            v((B, D), BF16),
            dma((6,)),
            dma((S,)),
            dma((S,)),
            dma((S, 4)),
            dma((S,)),
            dma((S,)),
            dma((S,)),
            dma((S,)),
            dma((S,)),
            dma((S,)),
            dma((S,)),
            dma((S,)),
            dma((S,)),
            dma((S,)),
            dma((5,)),
            dma((5,)),
        ],
        compiler_params=pltpu.CompilerParams(
            collective_id=0, has_side_effects=True, vmem_limit_bytes=VMEM_BYTES
        ),
        name="swivel",
    )(
        row_emb,
        col_emb,
        counts,
        row_totals.reshape(8, L),
        col_totals.reshape(8, L),
        row_ids.reshape(S, NO * B // L, L),
        col_ids,
    )
    return pl.pallas_call(
        finish,
        out_shape=(jax.ShapeDtypeStruct((B, D), F32), jax.ShapeDtypeStruct((B, D), F32)),
        in_specs=[hbm, hbm],
        out_specs=(hbm, hbm),
        scratch_shapes=[
            v((B, D), F32),
            v((B, D), BF16),
            v((B, D), F32),
            dma((PIECES, 4)),
        ],
        name="finish",
    )(rows, cols)


def solution(mesh):
    in_specs = (
        P("row", None),
        P("col", None),
        P(None, "row", "col"),
        P("row"),
        P("col"),
        P(),
        P(None, "col"),
    )
    out_specs = (P("row", None), P("col", None))
    return jax.shard_map(local, mesh=mesh, in_specs=in_specs, out_specs=out_specs, check_vma=False)
```

```python
import functools
import math

import jax
import jax.numpy as jnp
from jax import lax
from jax.experimental import pallas as pl
from jax.experimental.pallas import tpu as pltpu
from jax.sharding import PartitionSpec as P

MESH = pl.DeviceIdType.MESH
F32 = jnp.float32
BF16 = jnp.bfloat16
LOG_TOTAL = 8.0

S = 2
B = 1024
D = 256
NO = 32
NC = 8
T = 256
L = 128
PIECES = 4
PARTS = (((0, 1), (1, 2), (2, 4)), ((0, 4),))
VMEM_BYTES = 57 * 1024 * 1024


def iota(shape, dim):
    return lax.broadcasted_iota(jnp.int32, shape, dim)


def nt(a, b):
    return lax.dot_general(a, b, (((1,), (1,)), ((), ())), preferred_element_type=F32)


def ds(start, size):
    return pl.ds(pl.multiple_of(start, size), size)


def turn(t):
    return jnp.where(t == 0, 2, jnp.where(t == 1, 1, t + 1))


def kernel(
    scale,
    row_emb_hbm,
    col_emb_hbm,
    counts,
    row_tot_hbm,
    col_tot_hbm,
    rid_hbm,
    cid_hbm,
    out_rows,
    out_cols,
    row_emb,
    col_emb,
    row_tot,
    col_tot,
    rid,
    cid_in,
    cnt,
    idxcol,
    cid,
    want,
    want2,
    send,
    recv,
    logsend,
    logrecv,
    sorter,
    unsort,
    cols,
    rl,
    cl,
    score,
    wgt,
    rowterm,
    rowown,
    r1recv,
    r2send,
    r2recv,
    r3x,
    r3send,
    big,
    xs,
    oh2,
    ohc,
    colt,
    gcol,
    c2send,
    c2recv,
    hacc,
    c3send,
    c3recv,
    c4buf,
    colg,
    in_sem,
    cnt_sem,
    f_send,
    f_recv,
    l_send,
    l_recv,
    r1_send,
    r1_recv,
    r2_send,
    r2_recv,
    r3_send,
    r3_recv,
    r4_send,
    r4_recv,
    c_send,
    c_recv,
):
    me = lax.axis_index("row")
    c = lax.axis_index("col")
    core = lax.rem(me, 2)
    x = lax.rem(lax.div(me, 2), 4)
    zl = lax.div(me, 8)
    zh = lax.div(c, 4)
    y = lax.rem(c, 4)
    z = zh * 4 + zl
    pair = me + 1 - 2 * core
    other = (1 - zh) * 4 + y

    def row_of(zl_, x_, core_):
        return (zl_ * 4 + x_) * 2 + core_

    def each_ring_peer(body):
        for group, dz in enumerate((0, 1, 7, 2 + 4 * core)):
            z2 = lax.rem(z + dz, 8)
            col = lax.div(z2, 4) * 4 + y
            first = lax.rem(z2, 4) * 8

            def one(rest, carry, col=col, first=first):
                body(first + jnp.bitwise_and(x * 2 + core + rest, 7), col)
                return carry

            lax.fori_loop(1 if group == 0 else 0, 8, one, 0)

    def remote(src, dst, send_sem, recv_sem, row, col):
        return pltpu.make_async_remote_copy(
            src_ref=src,
            dst_ref=dst,
            send_sem=send_sem,
            recv_sem=recv_sem,
            device_id={"row": row, "col": col},
            device_id_type=MESH,
        )

    def wait_bytes(ref, sem):
        pltpu.make_async_copy(ref, ref, sem).wait()

    loads = [
        pltpu.make_async_copy(src, dst, in_sem.at[k])
        for k, (src, dst) in enumerate(
            (
                (rid_hbm, rid),
                (row_tot_hbm, row_tot),
                (cid_hbm, cid_in),
                (col_tot_hbm, col_tot),
                (row_emb_hbm, row_emb),
                (col_emb_hbm, col_emb),
            )
        )
    ]
    for load in loads:
        load.start()
    for s in range(S):
        pltpu.make_async_copy(counts.at[s], cnt.at[s], cnt_sem.at[s]).start()

    barrier = pltpu.get_barrier_semaphore()

    def signal(row, col):
        pl.semaphore_signal(
            barrier, inc=1, device_id={"row": row, "col": col}, device_id_type=MESH
        )

    def greet(d, carry):
        z2 = lax.rem(z + lax.div(d, 8) + 6, 8)
        x2 = lax.rem(x + lax.rem(lax.div(d, 2), 4), 4)
        core2 = lax.rem(core + lax.rem(d, 2), 2)
        signal(row_of(lax.rem(z2, 4), x2, core2), lax.div(z2, 4) * 4 + y)
        return carry

    lax.fori_loop(0, 16, greet, 0)
    lax.fori_loop(17, 40, greet, 0)
    for d in range(1, 4):
        signal(me, zh * 4 + lax.rem(y + d, 4))
        signal(row_of(lax.rem(zl + d, 4), x, core), c)
    signal(me, other)

    lane = iota((T, L), 1)
    sub = iota((T, L), 0)

    lane1 = iota((L, L), 1)
    sub1 = iota((L, L), 0)
    pick = jnp.where(sub1 == lax.rem(lane1, 4) * NO + me, 1.0, 0.0).astype(BF16)
    lane2 = iota((32, L), 1)
    sub2 = iota((32, L), 0)
    eighth = (
        lax.rem(y + turn(lax.div(lax.rem(lane2, 32), 8)), 4) * 2
        + lax.div(lax.rem(lane2, 8), 4)
    )
    mask_want = jnp.where(
        (lax.div(sub2, 8) == lax.div(lane2, 32)) & (lax.rem(sub2, 8) == eighth), 1.0, 0.0
    )
    mask_want2 = jnp.where(iota((16, 1, L), 0) == lax.div(iota((16, 1, L), 2), 8), 1.0, 0.0)
    low_half = lax.rem(iota((1, L), 1), 8) < 4
    for load in loads[:4]:
        load.wait()
    for s in range(S):
        ids = rid[:, s, :] - me * B
        high = jnp.right_shift(ids, 5).astype(F32).astype(BF16)
        low = jnp.bitwise_and(ids, 31).astype(F32).astype(BF16)
        picked_ids = 32.0 * jnp.dot(high, pick, preferred_element_type=F32) + jnp.dot(
            low, pick, preferred_element_type=F32
        )
        want[s] = jnp.sum(picked_ids.reshape(8, 32, L) * mask_want[None], axis=1)
        by_eighth = jnp.sum(picked_ids.reshape(2, 16, 8, L) * mask_want2[None], axis=1)
        for q in range(4):
            for half in range(2):
                want2[s, q * 2 + half : q * 2 + half + 1, :] = jnp.where(
                    low_half,
                    by_eighth[half, 2 * q : 2 * q + 1, :],
                    by_eighth[half, 2 * q + 1 : 2 * q + 2, :],
                ).astype(jnp.int32)
        cid[s] = (
            jnp.concatenate(
                [cid_in[s : s + 1, t * L : (t + 1) * L] for t in range(B // L)], axis=0
            )
            - c * B
        )

    def fill_idx(ids):
        for b in range(8):
            idxcol[b * L : (b + 1) * L, :] = jnp.broadcast_to(ids[b : b + 1, :], (L, L)).T.astype(
                jnp.int32
            )

    def gather_tile(i, table, logs):
        ids = idxcol[ds(i * T, T), :]
        parts = []
        total = None
        for t in range(B // L):
            hit = ids == lane + t * L
            parts.append(jnp.where(hit, 1.0, 0.0).astype(BF16))
            entry = jnp.where(hit, logs[t : t + 1, :], 0.0)
            total = entry if total is None else total + entry
        onehot = jnp.concatenate(parts, axis=1)
        picked = jnp.dot(onehot, table[...], preferred_element_type=F32)
        return picked, jnp.sum(total, axis=1, keepdims=True), onehot

    row_logs = jnp.log(row_tot[...].astype(F32)).astype(BF16).astype(F32)
    col_logs = jnp.log(col_tot[...].astype(F32))

    def make_send(s):
        fill_idx(want[s])

        def tile(i, carry):
            picked, column, _ = gather_tile(i, row_emb, row_logs)
            picked = picked.reshape(32, 8, D)
            packed = jnp.concatenate([picked[:, :, :L], picked[:, :, L:]], axis=1).astype(BF16)
            send[s, ds(i * 8, 8)] = packed.reshape(8, 4, 16, L)
            spread = jnp.where(lane == lax.rem(sub, 32), column, 0.0).reshape(8, 32, L)
            logsend[s, ds(i * 8, 8)] = jnp.sum(spread, axis=1, keepdims=True)
            return carry

        lax.fori_loop(0, B // T, tile, 0)

    def start_fetch(s):
        each_ring_peer(
            lambda row, col: remote(
                logsend.at[s, row], logrecv.at[s, me], l_send.at[s], l_recv.at[s], row, col
            ).start()
        )
        pltpu.make_async_copy(logsend.at[s, me], logrecv.at[s, me], l_recv.at[s]).start()
        for k, (t0, t1) in enumerate(PARTS[s]):
            tiles = slice(t0, t1)
            each_ring_peer(
                lambda row, col, k=k, tiles=tiles: remote(
                    send.at[s, row, tiles],
                    recv.at[s, tiles, me],
                    f_send.at[s],
                    f_recv.at[s, k],
                    row,
                    col,
                ).start()
            )
            pltpu.make_async_copy(
                send.at[s, me, tiles], recv.at[s, tiles, me], f_recv.at[s, k]
            ).start()

    def make_cols(s):
        fill_idx(cid[s].astype(F32))

        def tile(i, carry):
            picked, column, onehot = gather_tile(i, col_emb, col_logs)
            ohc[s, ds(i * T, T), :] = onehot
            cols[s, ds(i * T, T), :] = picked.astype(BF16)
            spread = jnp.where(lane == lax.rem(sub, L), column, 0.0).reshape(2, L, L)
            cl[s, ds(i * 2, 2)] = jnp.broadcast_to(
                0.5 * jnp.sum(spread, axis=1, keepdims=True), (2, 8, L)
            )
            return carry

        lax.fori_loop(0, B // T, tile, 0)

    def make_row_logs(s):
        wait_bytes(logrecv.at[s], l_recv.at[s])
        arrived = jnp.concatenate(
            [logrecv[s].reshape(NO, L), jnp.zeros((L - NO, L), F32)], axis=0
        ).T
        spread = jnp.where(
            iota((NO, NO, L), 2) == iota((NO, NO, L), 1), arrived[:NO].reshape(NO, 1, L), 0.0
        )
        column = 0.5 * (jnp.sum(spread, axis=2, keepdims=True) - LOG_TOTAL)
        rl[s] = jnp.broadcast_to(column, (NO, NO, L)).reshape(B, L)

    def block_tile(s, t):
        i = lax.rem(y + turn(t), 4)
        for k, (t0, t1) in enumerate(PARTS[s]):

            @pl.when(t == t0)
            def _(k=k, t0=t0, t1=t1):
                wait_bytes(recv.at[s, t0:t1], f_recv.at[s, k])

        arrived = jnp.dot(
            unsort[...], recv[s, t].reshape(512, L), preferred_element_type=F32
        ).astype(BF16)
        rows = jnp.concatenate([arrived[:T], arrived[T:]], axis=1)
        score[...] = nt(rows * jnp.bfloat16(0.5), cols[s])

        def chunk(k, carry):
            at = ds(k * 32, 32)
            here = ds(i * T + k * 32, 32)
            row_part = rl[s, ds(t * T + k * 32, 32), :].reshape(4, 8, L)
            for t8 in range(B // L):
                lanes = slice(t8 * L, (t8 + 1) * L)
                count = cnt[s, here, lanes].reshape(4, 8, L)
                counted = jnp.maximum(count.astype(F32), 1.0)
                half = score[at, lanes].reshape(4, 8, L) + (row_part + cl[s, t8][None])
                fitted = (0.2 * scale + (0.5 * scale) * (counted * lax.rsqrt(counted))) * (
                    half - (0.5 * math.log(2.0)) * jnp.log2(counted)
                )
                hinge = 0.5 * scale + (0.5 * scale) * jnp.tanh(half)
                weight = jnp.where(count > 0, fitted, hinge).reshape(32, L)
                wgt[at, lanes] = weight.astype(BF16)
            return carry

        lax.fori_loop(0, T // 32, chunk, 0)
        weights = wgt[...]
        term = jnp.dot(weights, cols[s], preferred_element_type=F32)
        colt[s] += jnp.dot(rows.T, weights, preferred_element_type=F32)
        rowterm[s, ds(i * T, T), :] = term.astype(BF16)

        @pl.when(t < 3)
        def _():
            remote(
                rowterm.at[s, ds(i * T, T), :],
                r1recv.at[s, t],
                r1_send.at[s],
                r1_recv.at[s],
                me,
                zh * 4 + i,
            ).start()

        @pl.when(t == 3)
        def _():
            rowown[...] = term

    def scatter_cols():
        first = colt[0].astype(BF16)
        second = colt[1].astype(BF16)
        for n in range(B // T):
            lanes = slice(n * T, (n + 1) * T)
            part = jnp.dot(first, ohc[0, :, lanes], preferred_element_type=F32) + jnp.dot(
                second, ohc[1, :, lanes], preferred_element_type=F32
            )
            gcol[2 * n] = part[:, :L]
            gcol[2 * n + 1] = part[:, L:]

    def sum_over_y(s):
        wait_bytes(r1recv.at[s], r1_recv.at[s])
        total = rowown[...]
        for d in range(3):
            total = total + r1recv[s, d].astype(F32)
        r2send[s] = total.astype(BF16)
        remote(r2send.at[s], r2recv.at[s], r2_send.at[s], r2_recv.at[s], me, other).start()

    def to_owners(s):
        wait_bytes(r2recv.at[s], r2_recv.at[s])
        mine = (r2send[s].astype(F32) + r2recv[s].astype(F32)).astype(BF16)
        for h in range(2):
            r3x[h * T : (h + 1) * T, :] = mine[:, h * L : (h + 1) * L]
        r3send[s] = (
            jnp.dot(sorter[...], r3x[...], preferred_element_type=F32)
            .astype(BF16)
            .reshape(NO, 16, L)
        )

        each_ring_peer(
            lambda row, col: remote(
                r3send.at[s, row], big.at[s, y, me], r3_send.at[s], r3_recv.at[s], row, col
            ).start()
        )
        pltpu.make_async_copy(r3send.at[s, me], big.at[s, y, me], r3_recv.at[s]).start()

    def share_owned(s):
        wait_bytes(big.at[s, y], r3_recv.at[s])
        for d in range(1, 4):
            remote(
                big.at[s, y],
                big.at[s, y],
                r4_send.at[s],
                r4_recv.at[s],
                me,
                zh * 4 + lax.rem(y + d, 4),
            ).start()

    def make_oh2(s):
        def tile(i, carry):
            for t in range(B // L):
                hit = want2[s, t : t + 1, :] == sub + i * T
                oh2[s, ds(i * T, T), t * L : (t + 1) * L] = jnp.where(hit, 1.0, 0.0).astype(BF16)
            return carry

        lax.fori_loop(0, B // T, tile, 0)

    def add_rows(s):
        wait_bytes(big.at[s, 0:3], r4_recv.at[s])
        for q in range(4):
            entries = big[s, q].astype(F32).reshape(NO, 2, 8, L)
            for h in range(2):
                xs[q * T : (q + 1) * T, h * L : (h + 1) * L] = (
                    entries[:, h].reshape(T, L).astype(BF16)
                )

        def tile(i, carry):
            part = jnp.dot(oh2[s, ds(i * T, T), :], xs[...], preferred_element_type=F32)
            if s == 0:
                out_rows[ds(i * T, T), :] = part
            else:
                out_rows[ds(i * T, T), :] += part
            return carry

        lax.fori_loop(0, B // T, tile, 0)

    loads[4].wait()
    make_send(0)
    pl.semaphore_wait(barrier, 39 + 3 + 3 + 1)
    start_fetch(0)
    make_send(1)
    loads[5].wait()
    make_cols(0)
    order = iota((512, 512), 0)
    place = iota((512, 512), 1)
    sorter[...] = jnp.where(
        lax.rem(order, 16) * 32 + lax.div(order, 16) == place, 1.0, 0.0
    ).astype(BF16)
    unsort[...] = jnp.where(
        lax.rem(order, 32) * 16 + lax.div(order, 32) == place, 1.0, 0.0
    ).astype(BF16)
    colt[...] = jnp.zeros_like(colt)
    make_row_logs(0)
    wait_bytes(cnt.at[0], cnt_sem.at[0])

    def tile0(t, carry):
        block_tile(0, t)

        @pl.when(t == 0)
        def _():
            start_fetch(1)

        return carry

    lax.fori_loop(0, 4, tile0, 0)
    make_cols(1)
    make_row_logs(1)
    wait_bytes(cnt.at[1], cnt_sem.at[1])

    def tile1(t, carry):
        @pl.when(t == 1)
        def _():
            sum_over_y(0)

        block_tile(1, t)
        return carry

    lax.fori_loop(0, 4, tile1, 0)
    sum_over_y(1)
    to_owners(0)
    scatter_cols()

    c2send[...] = gcol[pl.ds(4 * (1 - core), 4)].astype(BF16)
    remote(c2send, c2recv, c_send.at[0], c_recv.at[0], pair, c).start()

    wait_bytes(c2recv, c_recv.at[0])
    hacc[...] = gcol[pl.ds(4 * core, 4)] + c2recv[...].astype(F32)
    c3send[...] = hacc[...].astype(BF16)
    for d in range(1, 4):
        to = lax.rem(x + d, 4)
        remote(
            c3send.at[to], c3recv.at[d - 1], c_send.at[1], c_recv.at[1], row_of(zl, to, core), c
        ).start()
    make_oh2(0)
    make_oh2(1)
    to_owners(1)

    wait_bytes(c3recv, c_recv.at[1])
    c4buf[zl] = (
        hacc[x] + c3recv[0].astype(F32) + c3recv[1].astype(F32) + c3recv[2].astype(F32)
    ).astype(BF16)
    for d in range(1, 4):
        to = row_of(lax.rem(zl + d, 4), x, core)
        remote(c4buf.at[zl], c4buf.at[zl], c_send.at[2], c_recv.at[2], to, c).start()
    share_owned(0)

    wait_bytes(c4buf.at[0:3], c_recv.at[2])
    total = (c4buf[0].astype(F32) + c4buf[1].astype(F32)) + (
        c4buf[2].astype(F32) + c4buf[3].astype(F32)
    )
    quarter = ds(core * 512 + x * 128, 128)
    colg[quarter, :] = total.T.astype(BF16)
    for d in range(1, 4):
        to = row_of(zl, lax.rem(x + d, 4), core)
        remote(colg.at[quarter, :], colg.at[quarter, :], c_send.at[3], c_recv.at[3], to, c).start()
    share_owned(1)
    wait_bytes(colg.at[0:384, :], c_recv.at[3])
    half = ds(core * 512, 512)
    remote(colg.at[half, :], colg.at[half, :], c_send.at[4], c_recv.at[4], pair, c).start()
    add_rows(0)
    add_rows(1)
    wait_bytes(colg.at[half, :], c_recv.at[4])
    out_cols[...] = colg[...]

    for s in range(S):
        wait_bytes(send.at[s, 0 : NO - 1], f_send.at[s])
        wait_bytes(logsend.at[s, 0 : NO - 1], l_send.at[s])
        wait_bytes(r1recv.at[s], r1_send.at[s])
        wait_bytes(r2send.at[s], r2_send.at[s])
        wait_bytes(r3send.at[s, 0 : NO - 1], r3_send.at[s])
        wait_bytes(big.at[s, 0:3], r4_send.at[s])
    wait_bytes(c2send, c_send.at[0])
    wait_bytes(c3recv, c_send.at[1])
    wait_bytes(c4buf.at[0:3], c_send.at[2])
    wait_bytes(colg.at[0:384, :], c_send.at[3])
    wait_bytes(colg.at[0:512, :], c_send.at[4])


def finish(rows, cols, out_rows, out_cols, rows_buf, cols_buf, wide, sem):
    size = B // PIECES
    pieces = [pl.ds(k * size, size) for k in range(PIECES)]
    moves = []
    for k, at in enumerate(pieces):
        moves.append(
            (
                pltpu.make_async_copy(cols.at[at], cols_buf.at[at], sem.at[k, 0]),
                pltpu.make_async_copy(rows.at[at], rows_buf.at[at], sem.at[k, 1]),
                pltpu.make_async_copy(wide.at[at], out_cols.at[at], sem.at[k, 2]),
                pltpu.make_async_copy(rows_buf.at[at], out_rows.at[at], sem.at[k, 3]),
            )
        )
    for move in moves:
        move[0].start()
        move[1].start()
    for k, move in enumerate(moves):
        move[0].wait()
        wide[pieces[k], :] = cols_buf[pieces[k], :].astype(F32)
        move[2].start()
        move[1].wait()
        move[3].start()
    for move in moves:
        move[2].wait()
        move[3].wait()


def local(row_emb, col_emb, counts, row_totals, col_totals, row_ids, col_ids):
    scale = (S * math.sqrt(NO * B * NC * B)) ** (-0.5)
    vmem = pl.BlockSpec(memory_space=pltpu.VMEM)
    hbm = pl.BlockSpec(memory_space=pl.ANY)
    v = pltpu.VMEM
    dma = pltpu.SemaphoreType.DMA
    rows, cols = pl.pallas_call(
        functools.partial(kernel, scale),
        out_shape=(jax.ShapeDtypeStruct((B, D), F32), jax.ShapeDtypeStruct((B, D), BF16)),
        in_specs=[hbm] * 7,
        out_specs=(vmem, vmem),
        scratch_shapes=[
            v((B, D), BF16),
            v((B, D), BF16),
            v((8, L), jnp.int32),
            v((8, L), jnp.int32),
            v((NO * B // L, S, L), jnp.int32),
            v((S, B), jnp.int32),
            v((S, B, B), jnp.int32),
            v((B, L), jnp.int32),
            v((S, 8, L), jnp.int32),
            v((S, 8, L), F32),
            v((S, 8, L), jnp.int32),
            v((S, NO, 4, 16, L), BF16),
            v((S, 4, NO, 16, L), BF16),
            v((S, NO, 1, L), F32),
            v((S, NO, 1, L), F32),
            v((512, 512), BF16),
            v((512, 512), BF16),
            v((S, B, D), BF16),
            v((S, B, L), F32),
            v((S, 8, 8, L), F32),
            v((T, B), F32),
            v((T, B), BF16),
            v((S, B, D), BF16),
            v((T, D), F32),
            v((S, 3, T, D), BF16),
            v((S, T, D), BF16),
            v((S, T, D), BF16),
            v((512, L), BF16),
            v((S, NO, 16, L), BF16),
            v((S, 4, NO, 16, L), BF16),
            v((B, D), BF16),
            v((S, B, B), BF16),
            v((S, B, B), BF16),
            v((S, D, B), F32),
            v((8, D, L), F32),
            v((4, D, L), BF16),
            v((4, D, L), BF16),
            v((4, D, L), F32),
            v((4, D, L), BF16),
            v((3, D, L), BF16),
            v((4, D, L), BF16),
            v((B, D), BF16),
            dma((6,)),
            dma((S,)),
            dma((S,)),
            dma((S, 4)),
            dma((S,)),
            dma((S,)),
            dma((S,)),
            dma((S,)),
            dma((S,)),
            dma((S,)),
            dma((S,)),
            dma((S,)),
            dma((S,)),
            dma((S,)),
            dma((5,)),
            dma((5,)),
        ],
        compiler_params=pltpu.CompilerParams(
            collective_id=0, has_side_effects=True, vmem_limit_bytes=VMEM_BYTES
        ),
        name="swivel",
    )(
        row_emb,
        col_emb,
        counts,
        row_totals.reshape(8, L),
        col_totals.reshape(8, L),
        jnp.transpose(row_ids.reshape(S, NO * B // L, L), (1, 0, 2)),
        col_ids,
    )
    return pl.pallas_call(
        finish,
        out_shape=(jax.ShapeDtypeStruct((B, D), F32), jax.ShapeDtypeStruct((B, D), F32)),
        in_specs=[hbm, hbm],
        out_specs=(hbm, hbm),
        scratch_shapes=[
            v((B, D), F32),
            v((B, D), BF16),
            v((B, D), F32),
            dma((PIECES, 4)),
        ],
        name="finish",
    )(rows, cols)


def solution(mesh):
    in_specs = (
        P("row", None),
        P("col", None),
        P(None, "row", "col"),
        P("row"),
        P("col"),
        P(),
        P(None, "col"),
    )
    out_specs = (P("row", None), P("col", None))
    return jax.shard_map(local, mesh=mesh, in_specs=in_specs, out_specs=out_specs, check_vma=False)
```

```python
import functools
import math

import jax
import jax.numpy as jnp
from jax import lax
from jax.experimental import pallas as pl
from jax.experimental.pallas import tpu as pltpu
from jax.sharding import PartitionSpec as P

MESH = pl.DeviceIdType.MESH
F32 = jnp.float32
BF16 = jnp.bfloat16
LOG_TOTAL = 8.0

S = 2
B = 1024
D = 256
NO = 32
NC = 8
T = 256
L = 128
PIECES = 4
PARTS = (((0, 1), (1, 2), (2, 4)), ((0, 4),))
VMEM_BYTES = 57 * 1024 * 1024


def iota(shape, dim):
    return lax.broadcasted_iota(jnp.int32, shape, dim)


def nt(a, b):
    return lax.dot_general(a, b, (((1,), (1,)), ((), ())), preferred_element_type=F32)


def ds(start, size):
    return pl.ds(pl.multiple_of(start, size), size)


def turn(t):
    return jnp.where(t == 0, 2, jnp.where(t == 1, 1, t + 1))


def kernel(
    scale,
    row_emb_hbm,
    col_emb_hbm,
    counts,
    row_tot_hbm,
    col_tot_hbm,
    rid_hbm,
    cid_hbm,
    out_rows,
    out_cols,
    row_emb,
    col_emb,
    row_tot,
    col_tot,
    rid,
    cid_in,
    cnt,
    idxcol,
    cid,
    want,
    want2,
    send,
    recv,
    logsend,
    logrecv,
    sorter,
    unsort,
    cols,
    rl,
    cl,
    score,
    wgt,
    rowterm,
    rowown,
    r1recv,
    r2send,
    r2recv,
    r3x,
    r3send,
    big,
    xs,
    oh2,
    ohc,
    colt,
    gcol,
    c2send,
    c2recv,
    hacc,
    c3send,
    c3recv,
    c4buf,
    colg,
    in_sem,
    cnt_sem,
    f_send,
    f_recv,
    l_send,
    l_recv,
    r1_send,
    r1_recv,
    r2_send,
    r2_recv,
    r3_send,
    r3_recv,
    r4_send,
    r4_recv,
    c_send,
    c_recv,
):
    me = lax.axis_index("row")
    c = lax.axis_index("col")
    core = lax.rem(me, 2)
    x = lax.rem(lax.div(me, 2), 4)
    zl = lax.div(me, 8)
    zh = lax.div(c, 4)
    y = lax.rem(c, 4)
    z = zh * 4 + zl
    pair = me + 1 - 2 * core
    other = (1 - zh) * 4 + y

    def row_of(zl_, x_, core_):
        return (zl_ * 4 + x_) * 2 + core_

    def each_ring_peer(body):
        for group, dz in enumerate((0, 1, 7, 2 + 4 * core)):
            z2 = lax.rem(z + dz, 8)
            col = lax.div(z2, 4) * 4 + y
            first = lax.rem(z2, 4) * 8

            def one(rest, carry, col=col, first=first):
                body(first + jnp.bitwise_and(x * 2 + core + rest, 7), col)
                return carry

            lax.fori_loop(1 if group == 0 else 0, 8, one, 0)

    def remote(src, dst, send_sem, recv_sem, row, col):
        return pltpu.make_async_remote_copy(
            src_ref=src,
            dst_ref=dst,
            send_sem=send_sem,
            recv_sem=recv_sem,
            device_id={"row": row, "col": col},
            device_id_type=MESH,
        )

    def wait_bytes(ref, sem):
        pltpu.make_async_copy(ref, ref, sem).wait()

    loads = [
        pltpu.make_async_copy(src, dst, in_sem.at[k])
        for k, (src, dst) in enumerate(
            (
                (rid_hbm, rid),
                (row_tot_hbm, row_tot),
                (cid_hbm, cid_in),
                (col_tot_hbm, col_tot),
                (row_emb_hbm, row_emb),
                (col_emb_hbm, col_emb),
            )
        )
    ]
    for load in loads:
        load.start()
    for s in range(S):
        pltpu.make_async_copy(counts.at[s], cnt.at[s], cnt_sem.at[s]).start()

    barrier = pltpu.get_barrier_semaphore()

    def signal(row, col):
        pl.semaphore_signal(
            barrier, inc=1, device_id={"row": row, "col": col}, device_id_type=MESH
        )

    def greet(d, carry):
        z2 = lax.rem(z + lax.div(d, 8) + 6, 8)
        x2 = lax.rem(x + lax.rem(lax.div(d, 2), 4), 4)
        core2 = lax.rem(core + lax.rem(d, 2), 2)
        signal(row_of(lax.rem(z2, 4), x2, core2), lax.div(z2, 4) * 4 + y)
        return carry

    lax.fori_loop(0, 16, greet, 0)
    lax.fori_loop(17, 40, greet, 0)
    for d in range(1, 4):
        signal(me, zh * 4 + lax.rem(y + d, 4))
        signal(row_of(lax.rem(zl + d, 4), x, core), c)
    signal(me, other)

    lane = iota((T, L), 1)
    sub = iota((T, L), 0)

    lane1 = iota((L, L), 1)
    sub1 = iota((L, L), 0)
    pick = jnp.where(sub1 == lax.rem(lane1, 4) * NO + me, 1.0, 0.0).astype(BF16)
    lane2 = iota((32, L), 1)
    sub2 = iota((32, L), 0)
    eighth = (
        lax.rem(y + turn(lax.div(lax.rem(lane2, 32), 8)), 4) * 2
        + lax.div(lax.rem(lane2, 8), 4)
    )
    mask_want = jnp.where(
        (lax.div(sub2, 8) == lax.div(lane2, 32)) & (lax.rem(sub2, 8) == eighth), 1.0, 0.0
    )
    mask_want2 = jnp.where(iota((16, 1, L), 0) == lax.div(iota((16, 1, L), 2), 8), 1.0, 0.0)
    low_half = lax.rem(iota((1, L), 1), 8) < 4
    for load in loads[:4]:
        load.wait()
    for s in range(S):
        ids = rid[:, s, :] - me * B
        high = jnp.right_shift(ids, 5).astype(F32).astype(BF16)
        low = jnp.bitwise_and(ids, 31).astype(F32).astype(BF16)
        picked_ids = 32.0 * jnp.dot(high, pick, preferred_element_type=F32) + jnp.dot(
            low, pick, preferred_element_type=F32
        )
        want[s] = jnp.sum(picked_ids.reshape(8, 32, L) * mask_want[None], axis=1)
        by_eighth = jnp.sum(picked_ids.reshape(2, 16, 8, L) * mask_want2[None], axis=1)
        for q in range(4):
            for half in range(2):
                want2[s, q * 2 + half : q * 2 + half + 1, :] = jnp.where(
                    low_half,
                    by_eighth[half, 2 * q : 2 * q + 1, :],
                    by_eighth[half, 2 * q + 1 : 2 * q + 2, :],
                ).astype(jnp.int32)
        cid[s] = (
            jnp.concatenate(
                [cid_in[s : s + 1, t * L : (t + 1) * L] for t in range(B // L)], axis=0
            )
            - c * B
        )

    def fill_idx(ids):
        for b in range(8):
            idxcol[b * L : (b + 1) * L, :] = jnp.broadcast_to(ids[b : b + 1, :], (L, L)).T.astype(
                jnp.int32
            )

    def gather_tile(i, table, logs):
        ids = idxcol[ds(i * T, T), :]
        parts = []
        total = None
        for t in range(B // L):
            hit = ids == lane + t * L
            parts.append(jnp.where(hit, 1.0, 0.0).astype(BF16))
            entry = jnp.where(hit, logs[t : t + 1, :], 0.0)
            total = entry if total is None else total + entry
        onehot = jnp.concatenate(parts, axis=1)
        picked = jnp.dot(onehot, table[...], preferred_element_type=F32)
        return picked, jnp.sum(total, axis=1, keepdims=True), onehot

    row_logs = jnp.log(row_tot[...].astype(F32)).astype(BF16).astype(F32)
    col_logs = jnp.log(col_tot[...].astype(F32))

    def make_send(s):
        fill_idx(want[s])

        def tile(i, carry):
            picked, column, _ = gather_tile(i, row_emb, row_logs)
            picked = picked.reshape(32, 8, D)
            packed = jnp.concatenate([picked[:, :, :L], picked[:, :, L:]], axis=1).astype(BF16)
            send[s, ds(i * 8, 8)] = packed.reshape(8, 4, 16, L)
            spread = jnp.where(lane == lax.rem(sub, 32), column, 0.0).reshape(8, 32, L)
            logsend[s, ds(i * 8, 8)] = jnp.sum(spread, axis=1, keepdims=True)
            return carry

        lax.fori_loop(0, B // T, tile, 0)

    def start_fetch(s):
        each_ring_peer(
            lambda row, col: remote(
                logsend.at[s, row], logrecv.at[s, me], l_send.at[s], l_recv.at[s], row, col
            ).start()
        )
        pltpu.make_async_copy(logsend.at[s, me], logrecv.at[s, me], l_recv.at[s]).start()
        for k, (t0, t1) in enumerate(PARTS[s]):
            tiles = slice(t0, t1)
            each_ring_peer(
                lambda row, col, k=k, tiles=tiles: remote(
                    send.at[s, row, tiles],
                    recv.at[s, tiles, me],
                    f_send.at[s],
                    f_recv.at[s, k],
                    row,
                    col,
                ).start()
            )
            pltpu.make_async_copy(
                send.at[s, me, tiles], recv.at[s, tiles, me], f_recv.at[s, k]
            ).start()

    def make_cols(s):
        fill_idx(cid[s].astype(F32))

        def tile(i, carry):
            picked, column, onehot = gather_tile(i, col_emb, col_logs)
            ohc[s, ds(i * T, T), :] = onehot
            cols[s, ds(i * T, T), :] = picked.astype(BF16)
            spread = jnp.where(lane == lax.rem(sub, L), column, 0.0).reshape(2, L, L)
            cl[s, ds(i * 2, 2)] = jnp.broadcast_to(
                0.5 * jnp.sum(spread, axis=1, keepdims=True), (2, 8, L)
            )
            return carry

        lax.fori_loop(0, B // T, tile, 0)

    def make_row_logs(s):
        wait_bytes(logrecv.at[s], l_recv.at[s])
        arrived = jnp.concatenate(
            [logrecv[s].reshape(NO, L), jnp.zeros((L - NO, L), F32)], axis=0
        ).T
        spread = jnp.where(
            iota((NO, NO, L), 2) == iota((NO, NO, L), 1), arrived[:NO].reshape(NO, 1, L), 0.0
        )
        column = 0.5 * (jnp.sum(spread, axis=2, keepdims=True) - LOG_TOTAL)
        rl[s] = jnp.broadcast_to(column, (NO, NO, L)).reshape(B, L)

    def block_tile(s, t):
        i = lax.rem(y + turn(t), 4)
        for k, (t0, t1) in enumerate(PARTS[s]):

            @pl.when(t == t0)
            def _(k=k, t0=t0, t1=t1):
                wait_bytes(recv.at[s, t0:t1], f_recv.at[s, k])

        arrived = jnp.dot(
            unsort[...], recv[s, t].reshape(512, L), preferred_element_type=F32
        ).astype(BF16)
        rows = jnp.concatenate([arrived[:T], arrived[T:]], axis=1)
        score[...] = nt(rows * jnp.bfloat16(0.5), cols[s])

        def chunk(k, carry):
            at = ds(k * 32, 32)
            here = ds(i * T + k * 32, 32)
            row_part = rl[s, ds(t * T + k * 32, 32), :].reshape(4, 8, L)
            for t8 in range(B // L):
                lanes = slice(t8 * L, (t8 + 1) * L)
                count = cnt[s, here, lanes].reshape(4, 8, L)
                counted = jnp.maximum(count.astype(F32), 1.0)
                half = score[at, lanes].reshape(4, 8, L) + (row_part + cl[s, t8][None])
                fitted = (0.2 * scale + (0.5 * scale) * (counted * lax.rsqrt(counted))) * (
                    half - (0.5 * math.log(2.0)) * jnp.log2(counted)
                )
                hinge = 0.5 * scale + (0.5 * scale) * jnp.tanh(half)
                weight = jnp.where(count > 0, fitted, hinge).reshape(32, L)
                wgt[at, lanes] = weight.astype(BF16)
            return carry

        lax.fori_loop(0, T // 32, chunk, 0)
        weights = wgt[...]
        term = jnp.dot(weights, cols[s], preferred_element_type=F32)
        colt[s] += jnp.dot(rows.T, weights, preferred_element_type=F32)
        rowterm[s, ds(i * T, T), :] = term.astype(BF16)

        @pl.when(t < 3)
        def _():
            remote(
                rowterm.at[s, ds(i * T, T), :],
                r1recv.at[s, t],
                r1_send.at[s],
                r1_recv.at[s],
                me,
                zh * 4 + i,
            ).start()

        @pl.when(t == 3)
        def _():
            rowown[...] = term

    def scatter_cols():
        first = colt[0].astype(BF16)
        second = colt[1].astype(BF16)
        for n in range(B // T):
            lanes = slice(n * T, (n + 1) * T)
            part = jnp.dot(first, ohc[0, :, lanes], preferred_element_type=F32) + jnp.dot(
                second, ohc[1, :, lanes], preferred_element_type=F32
            )
            gcol[2 * n] = part[:, :L]
            gcol[2 * n + 1] = part[:, L:]

    def sum_over_y(s):
        wait_bytes(r1recv.at[s], r1_recv.at[s])
        total = rowown[...]
        for d in range(3):
            total = total + r1recv[s, d].astype(F32)
        r2send[s] = total.astype(BF16)
        remote(r2send.at[s], r2recv.at[s], r2_send.at[s], r2_recv.at[s], me, other).start()

    def to_owners(s):
        wait_bytes(r2recv.at[s], r2_recv.at[s])
        mine = (r2send[s].astype(F32) + r2recv[s].astype(F32)).astype(BF16)
        for h in range(2):
            r3x[h * T : (h + 1) * T, :] = mine[:, h * L : (h + 1) * L]
        r3send[s] = (
            jnp.dot(sorter[...], r3x[...], preferred_element_type=F32)
            .astype(BF16)
            .reshape(NO, 16, L)
        )

        each_ring_peer(
            lambda row, col: remote(
                r3send.at[s, row], big.at[s, y, me], r3_send.at[s], r3_recv.at[s], row, col
            ).start()
        )
        pltpu.make_async_copy(r3send.at[s, me], big.at[s, y, me], r3_recv.at[s]).start()

    def share_owned(s):
        wait_bytes(big.at[s, y], r3_recv.at[s])
        for d in (2, 1, 3):
            remote(
                big.at[s, y],
                big.at[s, y],
                r4_send.at[s],
                r4_recv.at[s],
                me,
                zh * 4 + lax.rem(y + d, 4),
            ).start()

    def make_oh2(s):
        def tile(i, carry):
            for t in range(B // L):
                hit = want2[s, t : t + 1, :] == sub + i * T
                oh2[s, ds(i * T, T), t * L : (t + 1) * L] = jnp.where(hit, 1.0, 0.0).astype(BF16)
            return carry

        lax.fori_loop(0, B // T, tile, 0)

    def add_rows(s):
        wait_bytes(big.at[s, 0:3], r4_recv.at[s])
        for q in range(4):
            entries = big[s, q].astype(F32).reshape(NO, 2, 8, L)
            for h in range(2):
                xs[q * T : (q + 1) * T, h * L : (h + 1) * L] = (
                    entries[:, h].reshape(T, L).astype(BF16)
                )

        def tile(i, carry):
            part = jnp.dot(oh2[s, ds(i * T, T), :], xs[...], preferred_element_type=F32)
            if s == 0:
                out_rows[ds(i * T, T), :] = part
            else:
                out_rows[ds(i * T, T), :] += part
            return carry

        lax.fori_loop(0, B // T, tile, 0)

    loads[4].wait()
    make_send(0)
    pl.semaphore_wait(barrier, 39 + 3 + 3 + 1)
    start_fetch(0)
    make_send(1)
    loads[5].wait()
    make_cols(0)
    order = iota((512, 512), 0)
    place = iota((512, 512), 1)
    sorter[...] = jnp.where(
        lax.rem(order, 16) * 32 + lax.div(order, 16) == place, 1.0, 0.0
    ).astype(BF16)
    unsort[...] = jnp.where(
        lax.rem(order, 32) * 16 + lax.div(order, 32) == place, 1.0, 0.0
    ).astype(BF16)
    colt[...] = jnp.zeros_like(colt)
    make_row_logs(0)
    wait_bytes(cnt.at[0], cnt_sem.at[0])
    start_fetch(1)

    def tile0(t, carry):
        block_tile(0, t)

        return carry

    lax.fori_loop(0, 4, tile0, 0)
    make_cols(1)
    make_row_logs(1)
    wait_bytes(cnt.at[1], cnt_sem.at[1])

    def tile1(t, carry):
        @pl.when(t == 1)
        def _():
            sum_over_y(0)

        block_tile(1, t)
        return carry

    lax.fori_loop(0, 4, tile1, 0)
    sum_over_y(1)
    to_owners(0)
    scatter_cols()

    c2send[...] = gcol[pl.ds(4 * (1 - core), 4)].astype(BF16)
    remote(c2send, c2recv, c_send.at[0], c_recv.at[0], pair, c).start()

    wait_bytes(c2recv, c_recv.at[0])
    hacc[...] = gcol[pl.ds(4 * core, 4)] + c2recv[...].astype(F32)
    c3send[...] = hacc[...].astype(BF16)
    for d in (2, 1, 3):
        to = lax.rem(x + d, 4)
        remote(
            c3send.at[to], c3recv.at[d - 1], c_send.at[1], c_recv.at[1], row_of(zl, to, core), c
        ).start()
    make_oh2(0)
    make_oh2(1)
    to_owners(1)

    wait_bytes(c3recv, c_recv.at[1])
    c4buf[zl] = (
        hacc[x] + c3recv[0].astype(F32) + c3recv[1].astype(F32) + c3recv[2].astype(F32)
    ).astype(BF16)
    for d in range(1, 4):
        to = row_of(lax.rem(zl + d, 4), x, core)
        remote(c4buf.at[zl], c4buf.at[zl], c_send.at[2], c_recv.at[2], to, c).start()
    share_owned(0)

    wait_bytes(c4buf.at[0:3], c_recv.at[2])
    total = (c4buf[0].astype(F32) + c4buf[1].astype(F32)) + (
        c4buf[2].astype(F32) + c4buf[3].astype(F32)
    )
    quarter = ds(core * 512 + x * 128, 128)
    colg[quarter, :] = total.T.astype(BF16)
    for d in (2, 1, 3):
        to = row_of(zl, lax.rem(x + d, 4), core)
        remote(colg.at[quarter, :], colg.at[quarter, :], c_send.at[3], c_recv.at[3], to, c).start()
    share_owned(1)
    wait_bytes(colg.at[0:384, :], c_recv.at[3])
    half = ds(core * 512, 512)
    remote(colg.at[half, :], colg.at[half, :], c_send.at[4], c_recv.at[4], pair, c).start()
    add_rows(0)
    add_rows(1)
    wait_bytes(colg.at[half, :], c_recv.at[4])
    out_cols[...] = colg[...]

    for s in range(S):
        wait_bytes(send.at[s, 0 : NO - 1], f_send.at[s])
        wait_bytes(logsend.at[s, 0 : NO - 1], l_send.at[s])
        wait_bytes(r1recv.at[s], r1_send.at[s])
        wait_bytes(r2send.at[s], r2_send.at[s])
        wait_bytes(r3send.at[s, 0 : NO - 1], r3_send.at[s])
        wait_bytes(big.at[s, 0:3], r4_send.at[s])
    wait_bytes(c2send, c_send.at[0])
    wait_bytes(c3recv, c_send.at[1])
    wait_bytes(c4buf.at[0:3], c_send.at[2])
    wait_bytes(colg.at[0:384, :], c_send.at[3])
    wait_bytes(colg.at[0:512, :], c_send.at[4])


def finish(rows, cols, out_rows, out_cols, rows_buf, cols_buf, wide, sem):
    size = B // PIECES
    pieces = [pl.ds(k * size, size) for k in range(PIECES)]
    moves = []
    for k, at in enumerate(pieces):
        moves.append(
            (
                pltpu.make_async_copy(cols.at[at], cols_buf.at[at], sem.at[k, 0]),
                pltpu.make_async_copy(rows.at[at], rows_buf.at[at], sem.at[k, 1]),
                pltpu.make_async_copy(wide.at[at], out_cols.at[at], sem.at[k, 2]),
                pltpu.make_async_copy(rows_buf.at[at], out_rows.at[at], sem.at[k, 3]),
            )
        )
    for move in moves:
        move[0].start()
        move[1].start()
    for k, move in enumerate(moves):
        move[0].wait()
        wide[pieces[k], :] = cols_buf[pieces[k], :].astype(F32)
        move[2].start()
        move[1].wait()
        move[3].start()
    for move in moves:
        move[2].wait()
        move[3].wait()


def local(row_emb, col_emb, counts, row_totals, col_totals, row_ids, col_ids):
    scale = (S * math.sqrt(NO * B * NC * B)) ** (-0.5)
    vmem = pl.BlockSpec(memory_space=pltpu.VMEM)
    hbm = pl.BlockSpec(memory_space=pl.ANY)
    v = pltpu.VMEM
    dma = pltpu.SemaphoreType.DMA
    rows, cols = pl.pallas_call(
        functools.partial(kernel, scale),
        out_shape=(jax.ShapeDtypeStruct((B, D), F32), jax.ShapeDtypeStruct((B, D), BF16)),
        in_specs=[hbm] * 7,
        out_specs=(vmem, vmem),
        scratch_shapes=[
            v((B, D), BF16),
            v((B, D), BF16),
            v((8, L), jnp.int32),
            v((8, L), jnp.int32),
            v((NO * B // L, S, L), jnp.int32),
            v((S, B), jnp.int32),
            v((S, B, B), jnp.int32),
            v((B, L), jnp.int32),
            v((S, 8, L), jnp.int32),
            v((S, 8, L), F32),
            v((S, 8, L), jnp.int32),
            v((S, NO, 4, 16, L), BF16),
            v((S, 4, NO, 16, L), BF16),
            v((S, NO, 1, L), F32),
            v((S, NO, 1, L), F32),
            v((512, 512), BF16),
            v((512, 512), BF16),
            v((S, B, D), BF16),
            v((S, B, L), F32),
            v((S, 8, 8, L), F32),
            v((T, B), F32),
            v((T, B), BF16),
            v((S, B, D), BF16),
            v((T, D), F32),
            v((S, 3, T, D), BF16),
            v((S, T, D), BF16),
            v((S, T, D), BF16),
            v((512, L), BF16),
            v((S, NO, 16, L), BF16),
            v((S, 4, NO, 16, L), BF16),
            v((B, D), BF16),
            v((S, B, B), BF16),
            v((S, B, B), BF16),
            v((S, D, B), F32),
            v((8, D, L), F32),
            v((4, D, L), BF16),
            v((4, D, L), BF16),
            v((4, D, L), F32),
            v((4, D, L), BF16),
            v((3, D, L), BF16),
            v((4, D, L), BF16),
            v((B, D), BF16),
            dma((6,)),
            dma((S,)),
            dma((S,)),
            dma((S, 4)),
            dma((S,)),
            dma((S,)),
            dma((S,)),
            dma((S,)),
            dma((S,)),
            dma((S,)),
            dma((S,)),
            dma((S,)),
            dma((S,)),
            dma((S,)),
            dma((5,)),
            dma((5,)),
        ],
        compiler_params=pltpu.CompilerParams(
            collective_id=0, has_side_effects=True, vmem_limit_bytes=VMEM_BYTES
        ),
        name="swivel",
    )(
        row_emb,
        col_emb,
        counts,
        row_totals.reshape(8, L),
        col_totals.reshape(8, L),
        jnp.transpose(row_ids.reshape(S, NO * B // L, L), (1, 0, 2)),
        col_ids,
    )
    return pl.pallas_call(
        finish,
        out_shape=(jax.ShapeDtypeStruct((B, D), F32), jax.ShapeDtypeStruct((B, D), F32)),
        in_specs=[hbm, hbm],
        out_specs=(hbm, hbm),
        scratch_shapes=[
            v((B, D), F32),
            v((B, D), BF16),
            v((B, D), F32),
            dma((PIECES, 4)),
        ],
        name="finish",
    )(rows, cols)


def solution(mesh):
    in_specs = (
        P("row", None),
        P("col", None),
        P(None, "row", "col"),
        P("row"),
        P("col"),
        P(),
        P(None, "col"),
    )
    out_specs = (P("row", None), P("col", None))
    return jax.shard_map(local, mesh=mesh, in_specs=in_specs, out_specs=out_specs, check_vma=False)
```

```python
import functools
import math

import jax
import jax.numpy as jnp
from jax import lax
from jax.experimental import pallas as pl
from jax.experimental.pallas import tpu as pltpu
from jax.sharding import PartitionSpec as P

MESH = pl.DeviceIdType.MESH
F32 = jnp.float32
BF16 = jnp.bfloat16
LOG_TOTAL = 8.0

S = 2
B = 1024
D = 256
NO = 32
NC = 8
T = 256
L = 128
PIECES = 4
PARTS = (((0, 1), (1, 2), (2, 4)), ((0, 4),))
VMEM_BYTES = 57 * 1024 * 1024


def iota(shape, dim):
    return lax.broadcasted_iota(jnp.int32, shape, dim)


def nt(a, b):
    return lax.dot_general(a, b, (((1,), (1,)), ((), ())), preferred_element_type=F32)


def ds(start, size):
    return pl.ds(pl.multiple_of(start, size), size)


def turn(t):
    return jnp.where(t == 0, 2, jnp.where(t == 1, 1, t + 1))


def kernel(
    scale,
    row_emb_hbm,
    col_emb_hbm,
    counts,
    row_tot_hbm,
    col_tot_hbm,
    rid_hbm,
    cid_hbm,
    out_rows_hbm,
    out_cols_hbm,
    out_rows,
    row_emb,
    col_emb,
    row_tot,
    col_tot,
    rid,
    cid_in,
    cnt,
    idxcol,
    cid,
    want,
    want2,
    send,
    recv,
    logsend,
    logrecv,
    sorter,
    unsort,
    cols,
    rl,
    cl,
    score,
    wgt,
    rowterm,
    rowown,
    r1recv,
    r2send,
    r2recv,
    r3x,
    r3send,
    big,
    xs,
    oh2,
    ohc,
    colt,
    gcol,
    c2send,
    c2recv,
    hacc,
    c3send,
    c3recv,
    c4buf,
    colg,
    out_sem,
    in_sem,
    cnt_sem,
    f_send,
    f_recv,
    l_send,
    l_recv,
    r1_send,
    r1_recv,
    r2_send,
    r2_recv,
    r3_send,
    r3_recv,
    r4_send,
    r4_recv,
    c_send,
    c_recv,
):
    me = lax.axis_index("row")
    c = lax.axis_index("col")
    core = lax.rem(me, 2)
    x = lax.rem(lax.div(me, 2), 4)
    zl = lax.div(me, 8)
    zh = lax.div(c, 4)
    y = lax.rem(c, 4)
    z = zh * 4 + zl
    pair = me + 1 - 2 * core
    other = (1 - zh) * 4 + y

    def row_of(zl_, x_, core_):
        return (zl_ * 4 + x_) * 2 + core_

    def each_ring_peer(body):
        for group, dz in enumerate((0, 1, 7, 2 + 4 * core)):
            z2 = lax.rem(z + dz, 8)
            col = lax.div(z2, 4) * 4 + y
            first = lax.rem(z2, 4) * 8

            def one(rest, carry, col=col, first=first):
                body(first + jnp.bitwise_and(x * 2 + core + rest, 7), col)
                return carry

            lax.fori_loop(1 if group == 0 else 0, 8, one, 0)

    def remote(src, dst, send_sem, recv_sem, row, col):
        return pltpu.make_async_remote_copy(
            src_ref=src,
            dst_ref=dst,
            send_sem=send_sem,
            recv_sem=recv_sem,
            device_id={"row": row, "col": col},
            device_id_type=MESH,
        )

    def wait_bytes(ref, sem):
        pltpu.make_async_copy(ref, ref, sem).wait()

    loads = [
        pltpu.make_async_copy(src, dst, in_sem.at[k])
        for k, (src, dst) in enumerate(
            (
                (rid_hbm, rid),
                (row_tot_hbm, row_tot),
                (cid_hbm, cid_in),
                (col_tot_hbm, col_tot),
                (row_emb_hbm, row_emb),
                (col_emb_hbm, col_emb),
            )
        )
    ]
    for load in loads:
        load.start()
    for s in range(S):
        pltpu.make_async_copy(counts.at[s], cnt.at[s], cnt_sem.at[s]).start()

    barrier = pltpu.get_barrier_semaphore()

    def signal(row, col):
        pl.semaphore_signal(
            barrier, inc=1, device_id={"row": row, "col": col}, device_id_type=MESH
        )

    def greet(d, carry):
        z2 = lax.rem(z + lax.div(d, 8) + 6, 8)
        x2 = lax.rem(x + lax.rem(lax.div(d, 2), 4), 4)
        core2 = lax.rem(core + lax.rem(d, 2), 2)
        signal(row_of(lax.rem(z2, 4), x2, core2), lax.div(z2, 4) * 4 + y)
        return carry

    lax.fori_loop(0, 16, greet, 0)
    lax.fori_loop(17, 40, greet, 0)
    for d in range(1, 4):
        signal(me, zh * 4 + lax.rem(y + d, 4))
        signal(row_of(lax.rem(zl + d, 4), x, core), c)
    signal(me, other)

    lane = iota((T, L), 1)
    sub = iota((T, L), 0)

    lane1 = iota((L, L), 1)
    sub1 = iota((L, L), 0)
    pick = jnp.where(sub1 == lax.rem(lane1, 4) * NO + me, 1.0, 0.0).astype(BF16)
    lane2 = iota((32, L), 1)
    sub2 = iota((32, L), 0)
    eighth = (
        lax.rem(y + turn(lax.div(lax.rem(lane2, 32), 8)), 4) * 2
        + lax.div(lax.rem(lane2, 8), 4)
    )
    mask_want = jnp.where(
        (lax.div(sub2, 8) == lax.div(lane2, 32)) & (lax.rem(sub2, 8) == eighth), 1.0, 0.0
    )
    mask_want2 = jnp.where(iota((16, 1, L), 0) == lax.div(iota((16, 1, L), 2), 8), 1.0, 0.0)
    low_half = lax.rem(iota((1, L), 1), 8) < 4
    for load in loads[:4]:
        load.wait()
    for s in range(S):
        ids = rid[:, s, :] - me * B
        high = jnp.right_shift(ids, 5).astype(F32).astype(BF16)
        low = jnp.bitwise_and(ids, 31).astype(F32).astype(BF16)
        picked_ids = 32.0 * jnp.dot(high, pick, preferred_element_type=F32) + jnp.dot(
            low, pick, preferred_element_type=F32
        )
        want[s] = jnp.sum(picked_ids.reshape(8, 32, L) * mask_want[None], axis=1)
        by_eighth = jnp.sum(picked_ids.reshape(2, 16, 8, L) * mask_want2[None], axis=1)
        for q in range(4):
            for half in range(2):
                want2[s, q * 2 + half : q * 2 + half + 1, :] = jnp.where(
                    low_half,
                    by_eighth[half, 2 * q : 2 * q + 1, :],
                    by_eighth[half, 2 * q + 1 : 2 * q + 2, :],
                ).astype(jnp.int32)
        cid[s] = (
            jnp.concatenate(
                [cid_in[s : s + 1, t * L : (t + 1) * L] for t in range(B // L)], axis=0
            )
            - c * B
        )

    def fill_idx(ids):
        for b in range(8):
            idxcol[b * L : (b + 1) * L, :] = jnp.broadcast_to(ids[b : b + 1, :], (L, L)).T.astype(
                jnp.int32
            )

    def gather_tile(i, table, logs):
        ids = idxcol[ds(i * T, T), :]
        parts = []
        total = None
        for t in range(B // L):
            hit = ids == lane + t * L
            parts.append(jnp.where(hit, 1.0, 0.0).astype(BF16))
            entry = jnp.where(hit, logs[t : t + 1, :], 0.0)
            total = entry if total is None else total + entry
        onehot = jnp.concatenate(parts, axis=1)
        picked = jnp.dot(onehot, table[...], preferred_element_type=F32)
        return picked, jnp.sum(total, axis=1, keepdims=True), onehot

    row_logs = jnp.log(row_tot[...].astype(F32)).astype(BF16).astype(F32)
    col_logs = jnp.log(col_tot[...].astype(F32))

    def make_send(s):
        fill_idx(want[s])

        def tile(i, carry):
            picked, column, _ = gather_tile(i, row_emb, row_logs)
            picked = picked.reshape(32, 8, D)
            packed = jnp.concatenate([picked[:, :, :L], picked[:, :, L:]], axis=1).astype(BF16)
            send[s, ds(i * 8, 8)] = packed.reshape(8, 4, 16, L)
            spread = jnp.where(lane == lax.rem(sub, 32), column, 0.0).reshape(8, 32, L)
            logsend[s, ds(i * 8, 8)] = jnp.sum(spread, axis=1, keepdims=True)
            return carry

        lax.fori_loop(0, B // T, tile, 0)

    def start_fetch(s):
        each_ring_peer(
            lambda row, col: remote(
                logsend.at[s, row], logrecv.at[s, me], l_send.at[s], l_recv.at[s], row, col
            ).start()
        )
        pltpu.make_async_copy(logsend.at[s, me], logrecv.at[s, me], l_recv.at[s]).start()
        for k, (t0, t1) in enumerate(PARTS[s]):
            tiles = slice(t0, t1)
            each_ring_peer(
                lambda row, col, k=k, tiles=tiles: remote(
                    send.at[s, row, tiles],
                    recv.at[s, tiles, me],
                    f_send.at[s],
                    f_recv.at[s, k],
                    row,
                    col,
                ).start()
            )
            pltpu.make_async_copy(
                send.at[s, me, tiles], recv.at[s, tiles, me], f_recv.at[s, k]
            ).start()

    def make_cols(s):
        fill_idx(cid[s].astype(F32))

        def tile(i, carry):
            picked, column, onehot = gather_tile(i, col_emb, col_logs)
            ohc[s, ds(i * T, T), :] = onehot
            cols[s, ds(i * T, T), :] = picked.astype(BF16)
            spread = jnp.where(lane == lax.rem(sub, L), column, 0.0).reshape(2, L, L)
            cl[s, ds(i * 2, 2)] = jnp.broadcast_to(
                0.5 * jnp.sum(spread, axis=1, keepdims=True), (2, 8, L)
            )
            return carry

        lax.fori_loop(0, B // T, tile, 0)

    def make_row_logs(s):
        wait_bytes(logrecv.at[s], l_recv.at[s])
        arrived = jnp.concatenate(
            [logrecv[s].reshape(NO, L), jnp.zeros((L - NO, L), F32)], axis=0
        ).T
        spread = jnp.where(
            iota((NO, NO, L), 2) == iota((NO, NO, L), 1), arrived[:NO].reshape(NO, 1, L), 0.0
        )
        column = 0.5 * (jnp.sum(spread, axis=2, keepdims=True) - LOG_TOTAL)
        rl[s] = jnp.broadcast_to(column, (NO, NO, L)).reshape(B, L)

    def block_tile(s, t):
        i = lax.rem(y + turn(t), 4)
        for k, (t0, t1) in enumerate(PARTS[s]):

            @pl.when(t == t0)
            def _(k=k, t0=t0, t1=t1):
                wait_bytes(recv.at[s, t0:t1], f_recv.at[s, k])

        arrived = jnp.dot(
            unsort[...], recv[s, t].reshape(512, L), preferred_element_type=F32
        ).astype(BF16)
        rows = jnp.concatenate([arrived[:T], arrived[T:]], axis=1)
        score[...] = nt(rows * jnp.bfloat16(0.5), cols[s])

        def chunk(k, carry):
            at = ds(k * 32, 32)
            here = ds(i * T + k * 32, 32)
            row_part = rl[s, ds(t * T + k * 32, 32), :].reshape(4, 8, L)
            for t8 in range(B // L):
                lanes = slice(t8 * L, (t8 + 1) * L)
                count = cnt[s, here, lanes].reshape(4, 8, L)
                counted = jnp.maximum(count.astype(F32), 1.0)
                half = score[at, lanes].reshape(4, 8, L) + (row_part + cl[s, t8][None])
                fitted = (0.2 * scale + (0.5 * scale) * (counted * lax.rsqrt(counted))) * (
                    half - (0.5 * math.log(2.0)) * jnp.log2(counted)
                )
                hinge = 0.5 * scale + (0.5 * scale) * jnp.tanh(half)
                weight = jnp.where(count > 0, fitted, hinge).reshape(32, L)
                wgt[at, lanes] = weight.astype(BF16)
            return carry

        lax.fori_loop(0, T // 32, chunk, 0)
        weights = wgt[...]
        term = jnp.dot(weights, cols[s], preferred_element_type=F32)
        colt[s] += jnp.dot(rows.T, weights, preferred_element_type=F32)
        rowterm[s, ds(i * T, T), :] = term.astype(BF16)

        @pl.when(t < 3)
        def _():
            remote(
                rowterm.at[s, ds(i * T, T), :],
                r1recv.at[s, t],
                r1_send.at[s],
                r1_recv.at[s],
                me,
                zh * 4 + i,
            ).start()

        @pl.when(t == 3)
        def _():
            rowown[...] = term

    def scatter_cols():
        first = colt[0].astype(BF16)
        second = colt[1].astype(BF16)
        for n in range(B // T):
            lanes = slice(n * T, (n + 1) * T)
            part = jnp.dot(first, ohc[0, :, lanes], preferred_element_type=F32) + jnp.dot(
                second, ohc[1, :, lanes], preferred_element_type=F32
            )
            gcol[2 * n] = part[:, :L]
            gcol[2 * n + 1] = part[:, L:]

    def sum_over_y(s):
        wait_bytes(r1recv.at[s], r1_recv.at[s])
        total = rowown[...]
        for d in range(3):
            total = total + r1recv[s, d].astype(F32)
        r2send[s] = total.astype(BF16)
        remote(r2send.at[s], r2recv.at[s], r2_send.at[s], r2_recv.at[s], me, other).start()

    def to_owners(s):
        wait_bytes(r2recv.at[s], r2_recv.at[s])
        mine = (r2send[s].astype(F32) + r2recv[s].astype(F32)).astype(BF16)
        for h in range(2):
            r3x[h * T : (h + 1) * T, :] = mine[:, h * L : (h + 1) * L]
        r3send[s] = (
            jnp.dot(sorter[...], r3x[...], preferred_element_type=F32)
            .astype(BF16)
            .reshape(NO, 16, L)
        )

        each_ring_peer(
            lambda row, col: remote(
                r3send.at[s, row], big.at[s, y, me], r3_send.at[s], r3_recv.at[s], row, col
            ).start()
        )
        pltpu.make_async_copy(r3send.at[s, me], big.at[s, y, me], r3_recv.at[s]).start()

    def share_owned(s):
        wait_bytes(big.at[s, y], r3_recv.at[s])
        for d in (2, 1, 3):
            remote(
                big.at[s, y],
                big.at[s, y],
                r4_send.at[s],
                r4_recv.at[s],
                me,
                zh * 4 + lax.rem(y + d, 4),
            ).start()

    def make_oh2(s):
        def tile(i, carry):
            for t in range(B // L):
                hit = want2[s, t : t + 1, :] == sub + i * T
                oh2[s, ds(i * T, T), t * L : (t + 1) * L] = jnp.where(hit, 1.0, 0.0).astype(BF16)
            return carry

        lax.fori_loop(0, B // T, tile, 0)

    def add_rows(s):
        wait_bytes(big.at[s, 0:3], r4_recv.at[s])
        for q in range(4):
            entries = big[s, q].astype(F32).reshape(NO, 2, 8, L)
            for h in range(2):
                xs[q * T : (q + 1) * T, h * L : (h + 1) * L] = (
                    entries[:, h].reshape(T, L).astype(BF16)
                )

        def tile(i, carry):
            part = jnp.dot(oh2[s, ds(i * T, T), :], xs[...], preferred_element_type=F32)
            if s == 0:
                out_rows[ds(i * T, T), :] = part
            else:
                out_rows[ds(i * T, T), :] += part
                at = ds(i * T, T)
                pltpu.make_async_copy(out_rows.at[at], out_rows_hbm.at[at], out_sem.at[i]).start()
            return carry

        lax.fori_loop(0, B // T, tile, 0)

    loads[4].wait()
    make_send(0)
    pl.semaphore_wait(barrier, 39 + 3 + 3 + 1)
    start_fetch(0)
    make_send(1)
    loads[5].wait()
    make_cols(0)
    order = iota((512, 512), 0)
    place = iota((512, 512), 1)
    sorter[...] = jnp.where(
        lax.rem(order, 16) * 32 + lax.div(order, 16) == place, 1.0, 0.0
    ).astype(BF16)
    unsort[...] = jnp.where(
        lax.rem(order, 32) * 16 + lax.div(order, 32) == place, 1.0, 0.0
    ).astype(BF16)
    colt[...] = jnp.zeros_like(colt)
    make_row_logs(0)
    wait_bytes(cnt.at[0], cnt_sem.at[0])
    start_fetch(1)

    def tile0(t, carry):
        block_tile(0, t)

        return carry

    lax.fori_loop(0, 4, tile0, 0)
    make_cols(1)
    make_row_logs(1)
    wait_bytes(cnt.at[1], cnt_sem.at[1])

    def tile1(t, carry):
        @pl.when(t == 1)
        def _():
            sum_over_y(0)

        block_tile(1, t)
        return carry

    lax.fori_loop(0, 4, tile1, 0)
    sum_over_y(1)
    to_owners(0)
    scatter_cols()

    c2send[...] = gcol[pl.ds(4 * (1 - core), 4)].astype(BF16)
    remote(c2send, c2recv, c_send.at[0], c_recv.at[0], pair, c).start()

    wait_bytes(c2recv, c_recv.at[0])
    hacc[...] = gcol[pl.ds(4 * core, 4)] + c2recv[...].astype(F32)
    c3send[...] = hacc[...].astype(BF16)
    for d in (2, 1, 3):
        to = lax.rem(x + d, 4)
        remote(
            c3send.at[to], c3recv.at[d - 1], c_send.at[1], c_recv.at[1], row_of(zl, to, core), c
        ).start()
    make_oh2(0)
    make_oh2(1)
    to_owners(1)

    wait_bytes(c3recv, c_recv.at[1])
    c4buf[zl] = (
        hacc[x] + c3recv[0].astype(F32) + c3recv[1].astype(F32) + c3recv[2].astype(F32)
    ).astype(BF16)
    for d in range(1, 4):
        to = row_of(lax.rem(zl + d, 4), x, core)
        remote(c4buf.at[zl], c4buf.at[zl], c_send.at[2], c_recv.at[2], to, c).start()
    share_owned(0)

    wait_bytes(c4buf.at[0:3], c_recv.at[2])
    total = (c4buf[0].astype(F32) + c4buf[1].astype(F32)) + (
        c4buf[2].astype(F32) + c4buf[3].astype(F32)
    )
    quarter = ds(core * 512 + x * 128, 128)
    colg[quarter, :] = total.T.astype(BF16)
    for d in (2, 1, 3):
        to = row_of(zl, lax.rem(x + d, 4), core)
        remote(colg.at[quarter, :], colg.at[quarter, :], c_send.at[3], c_recv.at[3], to, c).start()
    share_owned(1)
    wait_bytes(colg.at[0:384, :], c_recv.at[3])
    half = ds(core * 512, 512)
    remote(colg.at[half, :], colg.at[half, :], c_send.at[4], c_recv.at[4], pair, c).start()
    add_rows(0)
    add_rows(1)
    wait_bytes(colg.at[half, :], c_recv.at[4])
    cols_out = pltpu.make_async_copy(colg, out_cols_hbm, out_sem.at[4])
    cols_out.start()
    for i in range(B // T):
        at = slice(i * T, (i + 1) * T)
        pltpu.make_async_copy(out_rows.at[at], out_rows_hbm.at[at], out_sem.at[i]).wait()
    cols_out.wait()

    for s in range(S):
        wait_bytes(send.at[s, 0 : NO - 1], f_send.at[s])
        wait_bytes(logsend.at[s, 0 : NO - 1], l_send.at[s])
        wait_bytes(r1recv.at[s], r1_send.at[s])
        wait_bytes(r2send.at[s], r2_send.at[s])
        wait_bytes(r3send.at[s, 0 : NO - 1], r3_send.at[s])
        wait_bytes(big.at[s, 0:3], r4_send.at[s])
    wait_bytes(c2send, c_send.at[0])
    wait_bytes(c3recv, c_send.at[1])
    wait_bytes(c4buf.at[0:3], c_send.at[2])
    wait_bytes(colg.at[0:384, :], c_send.at[3])
    wait_bytes(colg.at[0:512, :], c_send.at[4])


def finish(rows, cols, out_rows, out_cols, rows_buf, cols_buf, wide, sem):
    size = B // PIECES
    pieces = [pl.ds(k * size, size) for k in range(PIECES)]
    moves = []
    for k, at in enumerate(pieces):
        moves.append(
            (
                pltpu.make_async_copy(cols.at[at], cols_buf.at[at], sem.at[k, 0]),
                pltpu.make_async_copy(rows.at[at], rows_buf.at[at], sem.at[k, 1]),
                pltpu.make_async_copy(wide.at[at], out_cols.at[at], sem.at[k, 2]),
                pltpu.make_async_copy(rows_buf.at[at], out_rows.at[at], sem.at[k, 3]),
            )
        )
    for move in moves:
        move[0].start()
        move[1].start()
    for k, move in enumerate(moves):
        move[0].wait()
        wide[pieces[k], :] = cols_buf[pieces[k], :].astype(F32)
        move[2].start()
        move[1].wait()
        move[3].start()
    for move in moves:
        move[2].wait()
        move[3].wait()


def local(row_emb, col_emb, counts, row_totals, col_totals, row_ids, col_ids):
    scale = (S * math.sqrt(NO * B * NC * B)) ** (-0.5)
    hbm = pl.BlockSpec(memory_space=pl.ANY)
    v = pltpu.VMEM
    dma = pltpu.SemaphoreType.DMA
    rows, cols = pl.pallas_call(
        functools.partial(kernel, scale),
        out_shape=(jax.ShapeDtypeStruct((B, D), F32), jax.ShapeDtypeStruct((B, D), BF16)),
        in_specs=[hbm] * 7,
        out_specs=(hbm, hbm),
        scratch_shapes=[
            v((B, D), F32),
            v((B, D), BF16),
            v((B, D), BF16),
            v((8, L), jnp.int32),
            v((8, L), jnp.int32),
            v((NO * B // L, S, L), jnp.int32),
            v((S, B), jnp.int32),
            v((S, B, B), jnp.int32),
            v((B, L), jnp.int32),
            v((S, 8, L), jnp.int32),
            v((S, 8, L), F32),
            v((S, 8, L), jnp.int32),
            v((S, NO, 4, 16, L), BF16),
            v((S, 4, NO, 16, L), BF16),
            v((S, NO, 1, L), F32),
            v((S, NO, 1, L), F32),
            v((512, 512), BF16),
            v((512, 512), BF16),
            v((S, B, D), BF16),
            v((S, B, L), F32),
            v((S, 8, 8, L), F32),
            v((T, B), F32),
            v((T, B), BF16),
            v((S, B, D), BF16),
            v((T, D), F32),
            v((S, 3, T, D), BF16),
            v((S, T, D), BF16),
            v((S, T, D), BF16),
            v((512, L), BF16),
            v((S, NO, 16, L), BF16),
            v((S, 4, NO, 16, L), BF16),
            v((B, D), BF16),
            v((S, B, B), BF16),
            v((S, B, B), BF16),
            v((S, D, B), F32),
            v((8, D, L), F32),
            v((4, D, L), BF16),
            v((4, D, L), BF16),
            v((4, D, L), F32),
            v((4, D, L), BF16),
            v((3, D, L), BF16),
            v((4, D, L), BF16),
            v((B, D), BF16),
            dma((5,)),
            dma((6,)),
            dma((S,)),
            dma((S,)),
            dma((S, 4)),
            dma((S,)),
            dma((S,)),
            dma((S,)),
            dma((S,)),
            dma((S,)),
            dma((S,)),
            dma((S,)),
            dma((S,)),
            dma((S,)),
            dma((S,)),
            dma((5,)),
            dma((5,)),
        ],
        compiler_params=pltpu.CompilerParams(
            collective_id=0, has_side_effects=True, vmem_limit_bytes=VMEM_BYTES
        ),
        name="swivel",
    )(
        row_emb,
        col_emb,
        counts,
        row_totals.reshape(8, L),
        col_totals.reshape(8, L),
        jnp.transpose(row_ids.reshape(S, NO * B // L, L), (1, 0, 2)),
        col_ids,
    )
    return pl.pallas_call(
        finish,
        out_shape=(jax.ShapeDtypeStruct((B, D), F32), jax.ShapeDtypeStruct((B, D), F32)),
        in_specs=[hbm, hbm],
        out_specs=(hbm, hbm),
        scratch_shapes=[
            v((B, D), F32),
            v((B, D), BF16),
            v((B, D), F32),
            dma((PIECES, 4)),
        ],
        name="finish",
    )(rows, cols)


def solution(mesh):
    in_specs = (
        P("row", None),
        P("col", None),
        P(None, "row", "col"),
        P("row"),
        P("col"),
        P(),
        P(None, "col"),
    )
    out_specs = (P("row", None), P("col", None))
    return jax.shard_map(local, mesh=mesh, in_specs=in_specs, out_specs=out_specs, check_vma=False)
```
